256 devices in a mesh: blk: 32 (over z, y_lo, core), axial: 8 (over x, y_hi).
Axes of the slice: x: 4, y: 4 (y_hi: 2, y_lo: 2; y = y_hi * 2 + y_lo), z: 8, core: 2. Of those that a mesh axis runs over, the one named last changes fastest.
Arguments:
- fields: float32 [5, 48, 256, 1024], P(None, None, 'blk', 'axial'), may hold values from -6 to 6
- inv_volume: float32 [48, 256, 1024], P(None, 'blk', 'axial'), may hold values from 0.5 to 2
- radius_ratio: float32 [48, 256, 1024], P(None, 'blk', 'axial'), may hold values from 58.09475 to 172.6007
- time_step: float32 [48, 256, 1024], P(None, 'blk', 'axial'), may hold values from 8 to 32
- jac_circ: float32 [5, 5], replicated, may hold values from -2.4 to 2.4
- jac_other: float32 [2, 5, 5], replicated, may hold values from -2.4 to 2.4
Outputs:
- advanced: float32 [5, 48, 256, 1024], P(None, None, 'blk', 'axial')
The draws below stay inside these ranges and needn't reach their ends.
All inputs are finite; a program needn't handle non-finite values.
Results may differ from the reference program's by a relative error of at most 0.0003.
Values sent between devices are 32-bit elements; how exact they have to be, the bound alone decides.
A program may use at most 64 MiB of HBM per device.

```python
import math
import jax
import jax.numpy as jnp
from jax import lax

NV = 5
KW = 48
NI = 256
NJ = 1024


def block_scale(own_key, dims, pieces, low, high):
    factor_of, own = 1.0, jax.random.fold_in(own_key, 6)
    for position, parts in pieces:
        heights = jnp.exp(jax.random.uniform(jax.random.fold_in(own, position), (parts,), jnp.float32, low / len(pieces), high / len(pieces)))
        factor_of = factor_of * jnp.repeat(heights, dims[position] // parts).reshape([-1 if axis == position else 1 for axis in range(len(dims))])
    return factor_of


def scatter_about(own_key, dims, scale, reach, cuts=(), kind=jnp.bfloat16):
    values = jax.random.normal(own_key, dims, jnp.float32) * scale
    if len(cuts) > 0:
        values = block_scale(own_key, dims, cuts, -0.22, 0.18) * values
    return jnp.clip(values, min=-reach, max=reach).astype(kind)


def setup_inputs(seed: int = 0) -> dict:
    key_of = jax.random.split(jax.random.key(seed), 7)
    fields = scatter_about(key_of[0], (NV, KW, NI, NJ), 1.0, 6.0, ((2, 32), (3, 8)), jnp.float32)
    inv_volume = jnp.clip(jnp.exp(math.log(2.0) - 1.3862944 * jax.random.uniform(key_of[1], (KW, NI, NJ), jnp.float32) ** block_scale(key_of[1], (KW, NI, NJ), ((1, 32), (2, 8)), -0.2, 0.2)), 0.5, 2.0)
    radius_ratio = jnp.clip(jnp.exp(math.log(172.6007) - 1.0889055 * jax.random.uniform(key_of[2], (KW, NI, NJ), jnp.float32) ** block_scale(key_of[2], (KW, NI, NJ), ((1, 32), (2, 8)), -0.2, 0.2)), 58.09475, 172.6007)
    time_step = jnp.clip(jnp.exp(math.log(32.0) - 1.3862944 * jax.random.uniform(key_of[3], (KW, NI, NJ), jnp.float32) ** block_scale(key_of[3], (KW, NI, NJ), ((1, 32), (2, 8)), -0.2, 0.2)), 8.0, 32.0)
    jac_circ = scatter_about(key_of[4], (NV, NV), 0.4, 2.4, (), jnp.float32)
    jac_other = scatter_about(key_of[5], (2, NV, NV), 0.4, 2.4, (), jnp.float32)
    return dict(fields=fields, inv_volume=inv_volume, radius_ratio=radius_ratio, time_step=time_step, jac_circ=jac_circ, jac_other=jac_other)


DISSIPATION = 0.03125
SECTION_ONE = 0.6
COURANT_RATIO = 2.0
SCALING_POWER = 2.0 / 3.0
HIGHEST = lax.Precision.HIGHEST


def coefficients(radius_ratio):
    scaled = COURANT_RATIO * (1.0 + jnp.power(radius_ratio, SCALING_POWER))
    return 0.25 * (scaled * scaled - 1.0)


def apply_matrix(matrix, operand):
    return jnp.einsum("vm,m...->v...", matrix, operand, precision=HIGHEST)


def cyclic_solve(lower_band, diagonal, upper_band, source):
    final_row = diagonal.shape[0] - 1
    corner_shift = -diagonal[0]
    top_right = lower_band[0]
    bottom_left = upper_band[final_row]
    modified = diagonal.at[0].add(-corner_shift).at[final_row].add(-top_right * bottom_left / corner_shift)
    spike_vec = jnp.zeros_like(diagonal).at[0].set(corner_shift).at[final_row].set(bottom_left)
    stacked = jnp.concatenate([source, spike_vec[None]], axis=0)
    lower_in = lower_band.at[0].set(0.0)
    upper_in = upper_band.at[final_row].set(0.0)

    def forward(carried, inputs):
        ratio_prev, value_prev = carried
        lower_now, diag_now, upper_now, source_now = inputs
        inverse = 1.0 / (diag_now - lower_now * ratio_prev)
        ratio_now = upper_now * inverse
        value_now = (source_now - lower_now * value_prev) * inverse
        return (ratio_now, value_now), (ratio_now, value_now)

    start_pair = (jnp.zeros_like(diagonal[0]), jnp.zeros_like(stacked[:, 0]))
    unused, (ratios, values) = lax.scan(forward, start_pair, (lower_in, modified, upper_in, jnp.moveaxis(stacked, 1, 0)))

    def backward(later_value, inputs):
        ratio_now, value_now = inputs
        result = value_now - ratio_now * later_value
        return result, result

    unused_two, solved = lax.scan(backward, jnp.zeros_like(values[0]), (ratios, values), reverse=True)
    plain_sol = solved[:, :-1]
    spike_sol = solved[:, -1]
    weight_top = top_right / corner_shift
    factor = (plain_sol[0] + weight_top * plain_sol[final_row]) / (1.0 + spike_sol[0] + weight_top * spike_sol[final_row])
    return jnp.moveaxis(plain_sol - spike_sol[:, None] * factor[None], 1, 0)


def layer_smoothed(fields, inv_volume, smoothing, jac_circ, jac_other, layer_at):
    height = fields.shape[1]
    centre = lax.dynamic_index_in_dim(fields, layer_at, 1, keepdims=False)
    beneath = lax.dynamic_index_in_dim(fields, jnp.maximum(layer_at - 1, 0), 1, keepdims=False)
    overhead = lax.dynamic_index_in_dim(fields, jnp.minimum(layer_at + 1, height - 1), 1, keepdims=False)
    volume_row = lax.dynamic_index_in_dim(inv_volume, layer_at, 0, keepdims=False)
    smooth_row = lax.dynamic_index_in_dim(smoothing, layer_at, 0, keepdims=False)
    diff_circ = (8.0 * (jnp.roll(centre, -1, 1) - jnp.roll(centre, 1, 1)) - (jnp.roll(centre, -2, 1) - jnp.roll(centre, 2, 1))) / 12.0
    padded = jnp.pad(centre, ((0, 0), (0, 0), (2, 2)))
    axial_count = centre.shape[2]

    def axial_at(offset):
        return padded[:, :, 2 + offset:2 + offset + axial_count]

    diff_axial = 0.5 * (axial_at(1) - axial_at(-1))
    diff_normal = 0.5 * (overhead - beneath)
    fourth = axial_at(2) - 4.0 * axial_at(1) + 6.0 * centre - 4.0 * axial_at(-1) + axial_at(-2)
    flux_sum = apply_matrix(jac_circ, diff_circ) + apply_matrix(jac_other[0], diff_axial) + apply_matrix(jac_other[1], diff_normal)
    residual_now = -volume_row[None] * (flux_sum + DISSIPATION * fourth)
    return cyclic_solve(-smooth_row, 1.0 + 2.0 * smooth_row, -smooth_row, residual_now)


def smoothed_all(fields, inv_volume, smoothing, jac_circ, jac_other):
    layer_ids = jnp.arange(fields.shape[1], dtype=jnp.int32)
    stacked = lax.map(lambda layer_at: layer_smoothed(fields, inv_volume, smoothing, jac_circ, jac_other, layer_at), layer_ids)
    return jnp.moveaxis(stacked, 0, 1)


def reference(fields, inv_volume, radius_ratio, time_step, jac_circ, jac_other):
    smoothing = coefficients(radius_ratio)
    section_one = fields + SECTION_ONE * time_step[None] * smoothed_all(fields, inv_volume, smoothing, jac_circ, jac_other)
    return fields + time_step[None] * smoothed_all(section_one, inv_volume, smoothing, jac_circ, jac_other)
```

```python
import functools

import jax
import jax.numpy as jnp
from jax import lax
from jax.experimental import pallas as pl
from jax.experimental.pallas import tpu as pltpu
from jax.sharding import Mesh
from jax.sharding import PartitionSpec as P

BLK = ("blk_0", "blk_1", "blk_2")
DISSIPATION = 0.03125
SECTION_ONE = 0.6
COURANT_RATIO = 2.0
SCALING_POWER = 2.0 / 3.0

NV = 5
TILES = 6
HALF = 3
ROWS = 8
SUB = 8
LANES = 128
UNITS = HALF * NV
F32 = jnp.float32


def kernel(
    nz,
    na,
    fields,
    inv_volume,
    radius_ratio,
    time_step,
    jac_c,
    jac_o,
    out,
    u1,
    u2,
    vol,
    rad,
    dt,
    wgt,
    cc,
    cp,
    yy,
    qrow,
    qhalo,
    pk,
    pkh,
    pb,
    pr,
    mb,
    rb,
    xb,
    xr,
    xx,
    gg,
    gr,
    gm,
    gt,
    td,
    tp,
    tx,
    res,
    in_sem,
    out_sem,
    circ_s,
    circ_r,
    ax_s,
    ax_r,
    q_s,
    q_r,
    gp_s,
    gp_r,
    ga_s,
    ga_r,
    pp_s,
    pp_r,
    pa_s,
    pa_r,
    xa_s,
    xa_r,
    xp_s,
    xp_r,
):
    ranks = nz * 2
    z = lax.axis_index("blk_0")
    y = lax.axis_index("blk_1")
    c = lax.axis_index("blk_2")
    a = lax.axis_index("axial")
    me = z * 2 + y

    def blk_device(b):
        return {"blk_0": b // 4, "blk_1": (b // 2) % 2, "blk_2": b % 2, "axial": a}

    def ax_device(index):
        return {"blk_0": z, "blk_1": y, "blk_2": c, "axial": index}

    def rank_device(rank):
        return {"blk_0": rank // 2, "blk_1": rank % 2, "blk_2": c, "axial": a}

    b = me * 2 + c
    size = ranks * 2
    right = blk_device((b + 1) % size)
    left = blk_device((b + size - 1) % size)
    ax_up = ax_device((a + 1) % na)
    ax_down = ax_device((a + na - 1) % na)
    partner = {"blk_0": z, "blk_1": y, "blk_2": 1 - c, "axial": a}
    hops = [dz for k in range(nz // 2, 0, -1) for dz in dict.fromkeys((k, nz - k))] + [0]
    offsets = [(dz, dy) for dz in hops for dy in (1, 0) if (dz, dy) != (0, 0)]

    def peer(n):
        dz, dy = offsets[n]
        return ((z + dz) % nz) * 2 + (y + dy) % 2

    def source(n):
        dz, dy = offsets[n]
        return ((z + nz - dz) % nz) * 2 + (y + dy) % 2

    def remote(src, dst, ssem, rsem, device):
        return pltpu.make_async_remote_copy(
            src_ref=src,
            dst_ref=dst,
            send_sem=ssem,
            recv_sem=rsem,
            device_id=device,
            device_id_type=pl.DeviceIdType.MESH,
        )

    loads = {
        "rad": [pltpu.make_async_copy(radius_ratio.at[:, i, :], rad.at[i + 1], in_sem.at[0, i]) for i in range(ROWS)],
        "vol": [pltpu.make_async_copy(inv_volume.at[:, i, :], vol.at[i], in_sem.at[1, i]) for i in range(ROWS)],
        "u": [pltpu.make_async_copy(fields.at[:, :, i, :], u1.at[:, i + 2], in_sem.at[2, i]) for i in range(ROWS)],
        "dt": [pltpu.make_async_copy(time_step.at[:, i, :], dt.at[i + 2], in_sem.at[3, i]) for i in range(ROWS)],
    }
    for name in ("u", "rad", "vol", "dt"):
        for copy in loads[name]:
            copy.start()

    barrier = pltpu.get_barrier_semaphore()
    greet = [left, right, ax_up, ax_down, partner] + [rank_device(peer(n)) for n in range(len(offsets))]
    for device in greet:
        pl.semaphore_signal(barrier, inc=1, device_id=device, device_id_type=pl.DeviceIdType.MESH)

    lane = lax.broadcasted_iota(jnp.int32, (SUB, LANES), 1)
    sub = lax.broadcasted_iota(jnp.int32, (SUB, LANES), 0)
    core0 = jnp.broadcast_to(c == 0, (SUB, LANES))

    def tile(t):
        return pl.ds(pl.multiple_of(t * SUB, SUB), SUB)

    def inverse_smoothing(ratio):
        scaled = COURANT_RATIO * (1.0 + jnp.exp(SCALING_POWER * jnp.log(ratio)))
        return 1.0 / (0.25 * (scaled * scaled - 1.0))

    def pack(u, t, slot):
        for half in range(2):
            packed = jnp.zeros((SUB, LANES), F32)
            for n in range(NV * ROWS // 2):
                flat = half * (NV * ROWS // 2) + n
                moved = pltpu.roll(u[flat // ROWS, flat % ROWS + 2, tile(t)], 4 * n + 2, 1)
                packed = jnp.where(lane // 4 == n, moved, packed)
            pk[slot, t, half] = packed

    for copy in loads["u"]:
        copy.wait()

    def pack_step(t, carry):
        pack(u1, t, 0)
        return carry

    lax.fori_loop(0, TILES, pack_step, 0)
    pl.semaphore_wait(barrier, len(greet))

    def circ_pair(ref, which, low, high, width, axis):
        def part(start):
            return ref.at[:, pl.ds(start, width)] if axis == 1 else ref.at[pl.ds(start, width)]

        count = ROWS
        to_left = remote(part(low), part(low + count), circ_s.at[which, 0], circ_r.at[which, 0], left)
        to_right = remote(part(low + count - width), part(low - width), circ_s.at[which, 1], circ_r.at[which, 1], right)
        return [to_left, to_right]

    def axial_pair(slot):
        up = remote(pk.at[slot], pkh.at[slot, 0], ax_s.at[slot, 0], ax_r.at[slot, 0], ax_up)
        down = remote(pk.at[slot], pkh.at[slot, 1], ax_s.at[slot, 1], ax_r.at[slot, 1], ax_down)
        return [up, down]

    pending = []

    def begin(copies):
        for copy in copies:
            copy.start()
        pending.extend(copies)
        return copies

    u_halo = begin(circ_pair(u1, 0, 2, 2, 2, 1))
    ax_halo = begin(axial_pair(0))
    for copy in loads["rad"] + loads["vol"]:
        copy.wait()

    def factor_step(t, carry):
        ratio = jnp.zeros((SUB, LANES), F32)
        product = jnp.ones((SUB, LANES), F32)
        first = jnp.zeros((SUB, LANES), F32)
        for i in range(ROWS):
            inverse = inverse_smoothing(rad[i + 1, tile(t)])
            wgt[i, tile(t)] = -vol[i, tile(t)] * inverse
            ratio = 1.0 / (2.0 + inverse - ratio)
            cc[i, tile(t)] = ratio
            previous = product
            product = product * ratio
            cp[i, tile(t)] = product
            first = first + previous * product
        gg[t, 0] = first
        gg[t, 1] = product
        gg[t, 2] = ratio
        return carry

    lax.fori_loop(0, TILES, factor_step, 0)
    other = 3 * (1 - c)
    mine = 3 * c
    g_pair = begin([remote(gg.at[pl.ds(other, HALF)], gr, gp_s, gp_r, partner)])
    for copy in loads["dt"]:
        copy.wait()
    rad_halo = begin(circ_pair(rad, 1, 1, 1, 1, 0))
    dt_halo = begin(circ_pair(dt, 2, 2, 2, 2, 0))

    def by_core(own, theirs):
        return jnp.where(core0, own, theirs), jnp.where(core0, theirs, own)

    def join(a_first, a_cross, a_last, b_first, b_cross, b_last):
        d = 1.0 / (1.0 - a_last * b_first)
        return (
            d,
            a_first + a_cross * a_cross * d * b_first,
            a_cross * d * b_cross,
            b_last + b_cross * b_cross * d * a_last,
        )

    def inner_pair(alpha, beta, a_last, b_first, d):
        return d * (alpha + a_last * beta), d * (beta + b_first * alpha)

    g_pair[0].wait_recv()

    def merge_step(t, carry):
        pairs = [by_core(gg[mine + t, n], gr[t, n]) for n in range(3)]
        (a_first, b_first), (a_cross, b_cross), (a_last, b_last) = pairs
        d, first, cross, last = join(a_first, a_cross, a_last, b_first, b_cross, b_last)
        for n, value in enumerate((a_cross, a_last, b_first, b_cross, d)):
            gm[1, t, n] = value
        for n, value in enumerate((first, cross, last)):
            gm[0, t, n] = value
        return carry

    lax.fori_loop(0, HALF, merge_step, 0)

    def spread(src_of, dst, ssem, rsem):
        for n in range(len(offsets)):
            target = peer(n)

            @pl.when(target < UNITS)
            def _(n=n, target=target):
                remote(src_of(target), dst.at[me], ssem.at[n], rsem.at[me], rank_device(target)).start()

    def spread_end(src_of, dst, ssem, rsem):
        for n in range(len(offsets)):
            target = peer(n)

            @pl.when(target < UNITS)
            def _(n=n, target=target):
                remote(src_of(target), dst.at[me], ssem.at[n], rsem.at[me], rank_device(target)).wait_send()

    def spread_recv(dst, rsem):
        for n in range(len(offsets)):
            origin = source(n)
            remote(dst.at[origin], dst.at[origin], rsem.at[origin], rsem.at[origin], rank_device(origin)).wait_recv()

    def g_source(target):
        return gm.at[0, target // NV, pl.ds(0, 3)]

    spread(g_source, gt, ga_s, ga_r)
    for copy in u_halo + ax_halo:
        copy.wait_recv()

    def splat(value):
        return jnp.broadcast_to(value, (SUB, LANES))

    def residual_step(u, slot, t, carry):
        edges = []
        low_edge = jnp.broadcast_to(a == 0, (SUB, LANES))
        high_edge = jnp.broadcast_to(a == na - 1, (SUB, LANES))
        for half in range(2):
            from_low = jnp.where(low_edge, 0.0, pkh[slot, 0, t, half])
            from_high = jnp.where(high_edge, 0.0, pkh[slot, 1, t, half])
            edges.append(jnp.where(lane % 4 < 2, from_low, from_high))
        above = jnp.minimum(t * SUB + SUB, TILES * SUB - 1)
        below = jnp.maximum(t * SUB - 1, 0)
        ahead = [jnp.zeros((SUB, LANES), F32)] * NV
        start = [jnp.zeros((SUB, LANES), F32)] * NV
        product = jnp.ones((SUB, LANES), F32)
        for i in range(ROWS):
            total = [None] * NV
            for m in range(NV):
                centre = u[m, i + 2, tile(t)]
                circ = (2.0 / 3.0) * (u[m, i + 3, tile(t)] - u[m, i + 1, tile(t)]) - (1.0 / 12.0) * (
                    u[m, i + 4, tile(t)] - u[m, i, tile(t)]
                )
                flat = m * ROWS + i
                half, n = flat // (NV * ROWS // 2), flat % (NV * ROWS // 2)
                edge = pltpu.roll(edges[half], LANES - (4 * n + 2), 1)
                plus1 = pltpu.roll(jnp.where(lane < 1, edge, centre), LANES - 1, 1)
                plus2 = pltpu.roll(jnp.where(lane < 2, edge, centre), LANES - 2, 1)
                minus1 = pltpu.roll(jnp.where(lane > LANES - 2, edge, centre), 1, 1)
                minus2 = pltpu.roll(jnp.where(lane > LANES - 3, edge, centre), 2, 1)
                axial = plus1 - minus1
                fourth = (plus2 + minus2) - 4.0 * (plus1 + minus1) + 6.0 * centre
                over = jnp.where(
                    sub == SUB - 1, splat(u[m, i + 2, pl.ds(above, 1)]), pltpu.roll(centre, SUB - 1, 0)
                )
                under = jnp.where(sub == 0, splat(u[m, i + 2, pl.ds(below, 1)]), pltpu.roll(centre, 1, 0))
                normal = over - under
                for v in range(NV):
                    term = jac_c[v, m] * circ + (0.5 * jac_o[0, v, m]) * axial + (0.5 * jac_o[1, v, m]) * normal
                    if v == m:
                        term = term + DISSIPATION * fourth
                    total[v] = term if total[v] is None else total[v] + term
            weight = wgt[i, tile(t)]
            ratio = cc[i, tile(t)]
            for v in range(NV):
                scaled = weight * total[v]
                if slot == 0 and i == 0:
                    qrow[0, v, tile(t)] = scaled
                if slot == 0 and i == ROWS - 1:
                    qrow[1, v, tile(t)] = scaled
                ahead[v] = (scaled + ahead[v]) * ratio
                yy[v, i, tile(t)] = ahead[v]
                start[v] = start[v] + product * ahead[v]
            product = cp[i, tile(t)]
        for v in range(NV):
            pb[slot, t, v, 0] = start[v]
            pb[slot, t, v, 1] = ahead[v]
        return carry

    def tree_factors():
        for r in range(ranks):
            for n in range(3):
                td[r, n] = gt[r, n]
        first, width, node = 0, ranks, ranks
        while width > 1:
            for k in range(0, width, 2):
                left_node, right_node = first + k, first + k + 1
                d, g0, g1, g2 = join(*(td[left_node, n] for n in range(3)), *(td[right_node, n] for n in range(3)))
                for n, value in enumerate((g0, g1, g2, d)):
                    td[node, n] = value
                node += 1
            first, width = first + width, width // 2
        top = 2 * ranks - 2
        inner = 1.0 - td[top, 1]
        td[top + 1, 0] = 1.0 / (inner * inner - td[top, 0] * td[top, 2])

    def tree_solve(slot):
        levels = []
        first, width, node = 0, ranks, ranks
        for r in range(ranks):
            for n in range(2):
                tp[r, n] = rb[slot, r, n]
        while width > 1:
            for k in range(0, width, 2):
                ln, rn = first + k, first + k + 1
                a0, b0 = inner_pair(tp[ln, 1], tp[rn, 0], td[ln, 2], td[rn, 0], td[node, 3])
                tp[node, 0] = tp[ln, 0] + td[ln, 1] * b0
                tp[node, 1] = tp[rn, 1] + td[rn, 1] * a0
                levels.append((node, ln, rn))
                node += 1
            first, width = first + width, width // 2
        top = 2 * ranks - 2
        inner = 1.0 - td[top, 1]
        det = td[top + 1, 0]
        tx[top, 0] = (inner * tp[top, 1] + td[top, 2] * tp[top, 0]) * det
        tx[top, 1] = (inner * tp[top, 0] + td[top, 0] * tp[top, 1]) * det
        for node, ln, rn in levels[::-1]:
            xl, xh = tx[node, 0], tx[node, 1]
            alpha = tp[ln, 1] + td[ln, 1] * xl
            beta = tp[rn, 0] + td[rn, 1] * xh
            mid_a, mid_b = inner_pair(alpha, beta, td[ln, 2], td[rn, 0], td[node, 3])
            tx[ln, 0] = xl
            tx[ln, 1] = mid_b
            tx[rn, 0] = mid_a
            tx[rn, 1] = xh
        for r in range(ranks):
            for n in range(2):
                xb[slot, r, n] = tx[r, n]

    def section(slot, u):
        lax.fori_loop(0, TILES, functools.partial(residual_step, u, slot), 0)
        pair = begin([remote(pb.at[slot, pl.ds(other, HALF)], pr.at[slot], pp_s.at[slot], pp_r.at[slot], partner)])
        pair[0].wait_recv()

        def merge(t, carry):
            a_cross, a_last, b_first, b_cross, d = (gm[1, t, n] for n in range(5))
            for v in range(NV):
                a_head, b_head = by_core(pb[slot, mine + t, v, 0], pr[slot, t, v, 0])
                a_tail, b_tail = by_core(pb[slot, mine + t, v, 1], pr[slot, t, v, 1])
                a0, b0 = inner_pair(a_tail, b_head, a_last, b_first, d)
                mb[slot, t * NV + v, 0] = a_head + a_cross * b0
                mb[slot, t * NV + v, 1] = b_tail + b_cross * a0
            return carry

        lax.fori_loop(0, HALF, merge, 0)
        spread(lambda target: mb.at[slot, target], rb.at[slot], pa_s.at[slot], pa_r.at[slot])

        q_halo = []
        if slot == 0:
            q_halo = begin(
                [
                    remote(qrow.at[0], qhalo.at[1], q_s.at[0], q_r.at[0], left),
                    remote(qrow.at[1], qhalo.at[0], q_s.at[1], q_r.at[1], right),
                ]
            )

        @pl.when(me < UNITS)
        def _():
            if slot == 0:
                gt[me] = gm[0, me // NV, pl.ds(0, 3)]
                spread_recv(gt, ga_r)
                tree_factors()
            rb[slot, me] = mb[slot, me]
            spread_recv(rb.at[slot], pa_r.at[slot])
            tree_solve(slot)
            xr[slot, me] = xb[slot, me]
            for n in range(len(offsets)):
                remote(
                    xb.at[slot, peer(n)], xr.at[slot, me], xa_s.at[slot, n], xa_r.at[slot, me], rank_device(peer(n))
                ).start()

        for n in range(len(offsets)):
            origin = source(n)

            @pl.when(origin < UNITS)
            def _(origin=origin):
                remote(
                    xr.at[slot, origin], xr.at[slot, origin], xa_r.at[slot, origin], xa_r.at[slot, origin], rank_device(origin)
                ).wait_recv()

        def unmerge(t, carry):
            a_cross, a_last, b_first, b_cross, d = (gm[1, t, n] for n in range(5))
            for v in range(NV):
                xl, xh = xr[slot, t * NV + v, 0], xr[slot, t * NV + v, 1]
                _, b_head = by_core(pb[slot, mine + t, v, 0], pr[slot, t, v, 0])
                a_tail, _ = by_core(pb[slot, mine + t, v, 1], pr[slot, t, v, 1])
                mid_a, mid_b = inner_pair(a_tail + a_cross * xl, b_head + b_cross * xh, a_last, b_first, d)
                xx[slot, mine + t, v, 0] = jnp.where(core0, xl, mid_a)
                xx[slot, mine + t, v, 1] = jnp.where(core0, mid_b, xh)
                res[slot, t, v, 0] = jnp.where(core0, mid_a, xl)
                res[slot, t, v, 1] = jnp.where(core0, xh, mid_b)
            return carry

        lax.fori_loop(0, HALF, unmerge, 0)
        back = begin(
            [remote(res.at[slot], xx.at[slot, pl.ds(mine, HALF)], xp_s.at[slot], xp_r.at[slot], partner)]
        )
        arrival = remote(res.at[slot], xx.at[slot, pl.ds(other, HALF)], xp_s.at[slot], xp_r.at[slot], partner)
        arrival.wait_recv()
        for copy in q_halo:
            copy.wait_recv()

    def sweep(slot, t, v):
        low, high = xx[slot, t, v, 0], xx[slot, t, v, 1]
        values = [None] * ROWS
        later = high
        for i in range(ROWS - 1, -1, -1):
            later = yy[v, i, tile(t)] + cp[i, tile(t)] * low + cc[i, tile(t)] * later
            values[i] = later
        return low, high, values

    section(0, u1)
    for copy in rad_halo + dt_halo:
        copy.wait_recv()

    def update_one(t, carry):
        diag_low = 2.0 + inverse_smoothing(rad[0, tile(t)])
        diag_high = 2.0 + inverse_smoothing(rad[ROWS + 1, tile(t)])
        for v in range(NV):
            low, high, values = sweep(0, t, v)
            low2 = diag_low * low - values[0] - qhalo[0, v, tile(t)]
            high2 = diag_high * high - values[ROWS - 1] - qhalo[1, v, tile(t)]
            for i, value in enumerate([low2, low] + values + [high, high2]):
                u2[v, i, tile(t)] = u1[v, i, tile(t)] + SECTION_ONE * dt[i, tile(t)] * value
        pack(u2, t, 1)
        return carry

    lax.fori_loop(0, TILES, update_one, 0)
    ax_halo = begin(axial_pair(1))
    for copy in ax_halo:
        copy.wait_recv()
    section(1, u2)

    def update_two(t, carry):
        for v in range(NV):
            _, _, values = sweep(1, t, v)
            for i, value in enumerate(values):
                u2[v, i + 2, tile(t)] = u1[v, i + 2, tile(t)] + dt[i + 2, tile(t)] * value
        return carry

    lax.fori_loop(0, TILES, update_two, 0)
    stores = [pltpu.make_async_copy(u2.at[:, i + 2], out.at[:, :, i, :], out_sem.at[i]) for i in range(ROWS)]
    for copy in stores:
        copy.start()
    for copy in pending:
        copy.wait_send()
    spread_end(g_source, gt, ga_s, ga_r)
    for slot in range(2):
        spread_end(lambda target, slot=slot: mb.at[slot, target], rb.at[slot], pa_s.at[slot], pa_r.at[slot])

        @pl.when(me < UNITS)
        def _(slot=slot):
            for n in range(len(offsets)):
                remote(
                    xb.at[slot, peer(n)], xr.at[slot, me], xa_s.at[slot, n], xa_r.at[slot, me], rank_device(peer(n))
                ).wait_send()

    for copy in stores:
        copy.wait()


def solution(mesh):
    count = mesh.shape["blk"]
    nz, na = count // 4, mesh.shape["axial"]
    split = Mesh(mesh.devices.reshape(nz, 2, 2, na), (*BLK, "axial"))
    ranks = nz * 2

    def on_device(fields, inv_volume, radius_ratio, time_step, jac_circ, jac_other):
        layers = fields.shape[1]
        vmem = lambda *shape: pltpu.VMEM(shape, F32)
        dma = lambda *shape: pltpu.SemaphoreType.DMA(shape)
        plane = (layers, LANES)
        cell = (SUB, LANES)
        peers = ranks - 1
        scratch = [
            vmem(NV, ROWS + 4, *plane),
            vmem(NV, ROWS + 4, *plane),
            vmem(ROWS, *plane),
            vmem(ROWS + 2, *plane),
            vmem(ROWS + 4, *plane),
            vmem(ROWS, *plane),
            vmem(ROWS, *plane),
            vmem(ROWS, *plane),
            vmem(NV, ROWS, *plane),
            vmem(2, NV, *plane),
            vmem(2, NV, *plane),
            vmem(2, TILES, 2, *cell),
            vmem(2, 2, TILES, 2, *cell),
            vmem(2, TILES, NV, 2, *cell),
            vmem(2, HALF, NV, 2, *cell),
            vmem(2, UNITS, 2, *cell),
            vmem(2, ranks, 2, *cell),
            vmem(2, ranks, 2, *cell),
            vmem(2, UNITS, 2, *cell),
            vmem(2, TILES, NV, 2, *cell),
            vmem(TILES, 3, *cell),
            vmem(HALF, 3, *cell),
            vmem(2, HALF, 5, *cell),
            vmem(ranks, 3, *cell),
            vmem(2 * ranks, 4, *cell),
            vmem(2 * ranks, 2, *cell),
            vmem(2 * ranks, 2, *cell),
            vmem(2, HALF, NV, 2, *cell),
            dma(4, ROWS),
            dma(ROWS),
            dma(3, 2),
            dma(3, 2),
            dma(2, 2),
            dma(2, 2),
            dma(2),
            dma(2),
            pltpu.SemaphoreType.DMA,
            pltpu.SemaphoreType.DMA,
            dma(peers),
            dma(ranks),
            dma(2),
            dma(2),
            dma(2, peers),
            dma(2, ranks),
            dma(2, peers),
            dma(2, ranks),
            dma(2),
            dma(2),
        ]
        anywhere = pl.BlockSpec(memory_space=pl.ANY)
        scalars = pl.BlockSpec(memory_space=pltpu.SMEM)
        return pl.pallas_call(
            functools.partial(kernel, nz, na),
            out_shape=jax.ShapeDtypeStruct(fields.shape, F32),
            in_specs=[anywhere] * 4 + [scalars] * 2,
            out_specs=anywhere,
            scratch_shapes=scratch,
            compiler_params=pltpu.CompilerParams(collective_id=0, has_side_effects=True),
        )(fields, inv_volume, radius_ratio, time_step, jac_circ, jac_other)

    return jax.shard_map(
        on_device,
        mesh=split,
        in_specs=(
            P(None, None, BLK, "axial"),
            P(None, BLK, "axial"),
            P(None, BLK, "axial"),
            P(None, BLK, "axial"),
            P(),
            P(),
        ),
        out_specs=P(None, None, BLK, "axial"),
        check_vma=False,
    )
```

```python
import functools

import jax
import jax.numpy as jnp
from jax import lax
from jax.experimental import pallas as pl
from jax.experimental.pallas import tpu as pltpu
from jax.sharding import Mesh
from jax.sharding import PartitionSpec as P

BLK = ("blk_0", "blk_1", "blk_2")
DISSIPATION = 0.03125
SECTION_ONE = 0.6
COURANT_RATIO = 2.0
SCALING_POWER = 2.0 / 3.0

NV = 5
TILES = 6
HALF = 3
ROWS = 8
SUB = 8
LANES = 128
UNITS = HALF * NV
F32 = jnp.float32


def kernel(
    nz,
    na,
    fields,
    inv_volume,
    radius_ratio,
    time_step,
    jac_c,
    jac_o,
    out,
    u1,
    u2,
    vol,
    rad,
    dt,
    wgt,
    cc,
    cp,
    yy,
    qrow,
    qhalo,
    pk,
    pkh,
    pb,
    pr,
    mb,
    rb,
    xb,
    xr,
    xx,
    gg,
    gr,
    gm,
    gt,
    td,
    tp,
    tx,
    res,
    tab,
    edge,
    in_sem,
    out_sem,
    uc_s,
    uc_r,
    circ_s,
    circ_r,
    ax_s,
    ax_r,
    q_s,
    q_r,
    gp_s,
    gp_r,
    ga_s,
    ga_r,
    pp_s,
    pp_r,
    pa_s,
    pa_r,
    xa_s,
    xa_r,
    xp_s,
    xp_r,
):
    ranks = nz * 2
    z = lax.axis_index("blk_0")
    y = lax.axis_index("blk_1")
    c = lax.axis_index("blk_2")
    a = lax.axis_index("axial")
    me = z * 2 + y

    def blk_device(b):
        return {"blk_0": b // 4, "blk_1": (b // 2) % 2, "blk_2": b % 2, "axial": a}

    def ax_device(index):
        return {"blk_0": z, "blk_1": y, "blk_2": c, "axial": index}

    def rank_device(rank):
        return {"blk_0": rank // 2, "blk_1": rank % 2, "blk_2": c, "axial": a}

    b = me * 2 + c
    size = ranks * 2
    right = blk_device((b + 1) % size)
    left = blk_device((b + size - 1) % size)
    ax_up = ax_device((a + 1) % na)
    ax_down = ax_device((a + na - 1) % na)
    partner = {"blk_0": z, "blk_1": y, "blk_2": 1 - c, "axial": a}
    hops = [dz for k in range(nz // 2, 0, -1) for dz in dict.fromkeys((k, nz - k))] + [0]
    offsets = [(dz, dy) for dz in hops for dy in (1, 0) if (dz, dy) != (0, 0)]

    def peer(n):
        dz, dy = offsets[n]
        return ((z + dz) % nz) * 2 + (y + dy) % 2

    def source(n):
        dz, dy = offsets[n]
        return ((z + nz - dz) % nz) * 2 + (y + dy) % 2

    def remote(src, dst, ssem, rsem, device):
        return pltpu.make_async_remote_copy(
            src_ref=src,
            dst_ref=dst,
            send_sem=ssem,
            recv_sem=rsem,
            device_id=device,
            device_id_type=pl.DeviceIdType.MESH,
        )

    loads = {
        "rad": [pltpu.make_async_copy(radius_ratio.at[:, i, :], rad.at[i + 1], in_sem.at[0, i]) for i in range(ROWS)],
        "vol": [pltpu.make_async_copy(inv_volume.at[:, i, :], vol.at[i], in_sem.at[1, i]) for i in range(ROWS)],
        "u": [pltpu.make_async_copy(fields.at[:, :, i, :], u1.at[:, i + 2], in_sem.at[2, i]) for i in range(ROWS)],
        "dt": [pltpu.make_async_copy(time_step.at[:, i, :], dt.at[i + 2], in_sem.at[3, i]) for i in range(ROWS)],
    }
    for name in ("u", "rad", "vol", "dt"):
        for copy in loads[name]:
            copy.start()

    barrier = pltpu.get_barrier_semaphore()
    greet = [left, right, ax_up, ax_down, partner] + [rank_device(peer(n)) for n in range(len(offsets))]
    for device in greet:
        pl.semaphore_signal(barrier, inc=1, device_id=device, device_id_type=pl.DeviceIdType.MESH)

    lane = lax.broadcasted_iota(jnp.int32, (SUB, LANES), 1)
    sub = lax.broadcasted_iota(jnp.int32, (SUB, LANES), 0)
    core0 = jnp.broadcast_to(c == 0, (SUB, LANES))

    def tile(t):
        return pl.ds(pl.multiple_of(t * SUB, SUB), SUB)

    def inverse_smoothing(ratio):
        scaled = COURANT_RATIO * (1.0 + jnp.exp(SCALING_POWER * jnp.log(ratio)))
        return 1.0 / (0.25 * (scaled * scaled - 1.0))

    def pack(u, t, carry):
        packed = list(carry)
        group = lane // 2 - t * ROWS
        for v in range(NV):
            for i in range(ROWS):
                moved = pltpu.roll(u[v, i + 2, tile(t)], 2 * (t * ROWS + i) + 2, 1)
                packed[v] = jnp.where(group == i, moved, packed[v])
                packed[NV + v] = jnp.where(group == i + 1, moved, packed[NV + v])
        return tuple(packed)

    def keep_packed(slot, packed):
        for v in range(NV):
            pk[slot, 0, v] = packed[v]
            pk[slot, 1, v] = packed[NV + v]

    blank = (jnp.zeros((SUB, LANES), F32),) * (2 * NV)

    for v in range(NV):
        for m in range(NV):
            tab[0, v, m] = jnp.broadcast_to(jac_c[v, m], (SUB, LANES))
            tab[1, v, m] = jnp.broadcast_to(0.5 * jac_o[v, 0, m], (SUB, LANES))
            tab[2, v, m] = jnp.broadcast_to(0.5 * jac_o[v, 1, m], (SUB, LANES))

    for copy in loads["u"]:
        copy.wait()

    keep_packed(0, lax.fori_loop(0, TILES, functools.partial(pack, u1), blank))
    pl.semaphore_wait(barrier, len(greet))

    def circ_pair(ref, which, low, width):
        def part(start):
            return ref.at[pl.ds(start, width)]

        count = ROWS
        to_left = remote(part(low), part(low + count), circ_s.at[which, 0], circ_r.at[which, 0], left)
        to_right = remote(part(low + count - width), part(low - width), circ_s.at[which, 1], circ_r.at[which, 1], right)
        return [to_left, to_right]

    def axial_pair(slot):
        up = remote(pk.at[slot, 0], pkh.at[slot, 0], ax_s.at[slot, 0], ax_r.at[slot, 0], ax_up)
        down = remote(pk.at[slot, 1], pkh.at[slot, 1], ax_s.at[slot, 1], ax_r.at[slot, 1], ax_down)
        return [up, down]

    def chunk_pair(t):
        def part(start):
            return u1.at[:, pl.ds(start, 2), tile(t)]

        to_left = remote(part(2), part(ROWS + 2), uc_s.at[0, t], uc_r.at[0, t], left)
        to_right = remote(part(ROWS), part(0), uc_s.at[1, t], uc_r.at[1, t], right)
        return [to_left, to_right]

    pending = []

    def begin(copies):
        for copy in copies:
            copy.start()
        pending.extend(copies)
        return copies

    other = HALF * (1 - c)
    mine = HALF * c

    def chunk_send(step, carry):
        for copy in chunk_pair((step + mine) % TILES):
            copy.start()
        return carry

    ax_halo = begin(axial_pair(0))
    lax.fori_loop(0, TILES, chunk_send, 0)
    for copy in loads["rad"] + loads["vol"]:
        copy.wait()

    def splat(value):
        return jnp.broadcast_to(value, (SUB, LANES))

    def local_step(u, slot, t, carry):
        above = jnp.minimum(t * SUB + SUB, TILES * SUB - 1)
        below = jnp.maximum(t * SUB - 1, 0)
        for i in range(ROWS):
            total = [None] * NV
            for m in range(NV):

                def row(k):
                    return u[m, k + 2, tile(t)] if slot == 1 or 0 <= k < ROWS else None

                def minus(p, q):
                    if p is None:
                        return -q
                    return p if q is None else p - q

                centre = u[m, i + 2, tile(t)]
                circ = (2.0 / 3.0) * minus(row(i + 1), row(i - 1)) - (1.0 / 12.0) * minus(row(i + 2), row(i - 2))
                plus1 = jnp.where(lane < LANES - 1, pltpu.roll(centre, LANES - 1, 1), 0.0)
                plus2 = jnp.where(lane < LANES - 2, pltpu.roll(centre, LANES - 2, 1), 0.0)
                minus1 = jnp.where(lane > 0, pltpu.roll(centre, 1, 1), 0.0)
                minus2 = jnp.where(lane > 1, pltpu.roll(centre, 2, 1), 0.0)
                axial = plus1 - minus1
                fourth = (plus2 + minus2) - 4.0 * (plus1 + minus1) + 6.0 * centre
                over = jnp.where(
                    sub == SUB - 1, splat(u[m, i + 2, pl.ds(above, 1)]), pltpu.roll(centre, SUB - 1, 0)
                )
                under = jnp.where(sub == 0, splat(u[m, i + 2, pl.ds(below, 1)]), pltpu.roll(centre, 1, 0))
                normal = over - under
                for v in range(NV):
                    term = tab[0, v, m] * circ + tab[1, v, m] * axial + tab[2, v, m] * normal
                    if v == m:
                        term = term + DISSIPATION * fourth
                    total[v] = term if total[v] is None else total[v] + term
            for v in range(NV):
                yy[v, i, tile(t)] = total[v]
        return carry

    def mix(which, values):
        out_values = []
        for v in range(NV):
            total = tab[which, v, 0] * values[0]
            for m in range(1, NV):
                total = total + tab[which, v, m] * values[m]
            out_values.append(total)
        return out_values

    def edge_fluxes(slot):
        even = lane % 2 == 0
        low_edge = jnp.broadcast_to(a == 0, (SUB, LANES))
        high_edge = jnp.broadcast_to(a == na - 1, (SUB, LANES))
        low = [jnp.where(low_edge, 0.0, pkh[slot, 0, v]) for v in range(NV)]
        high = [pltpu.roll(jnp.where(high_edge, 0.0, pkh[slot, 1, v]), LANES - 2, 1) for v in range(NV)]
        low_next = [pltpu.roll(value, LANES - 1, 1) for value in low]
        high_next = [pltpu.roll(value, 1, 1) for value in high]
        low_flux = mix(1, [jnp.where(even, -value, 0.0) for value in low_next])
        high_flux = mix(1, [jnp.where(even, 0.0, value) for value in high_next])
        for v in range(NV):
            low_total = low_flux[v] + DISSIPATION * jnp.where(even, low[v] - 4.0 * low_next[v], low[v])
            high_total = high_flux[v] + DISSIPATION * jnp.where(even, high[v], high[v] - 4.0 * high_next[v])
            for half in range(2):
                index = (lane // 4) * 2 + lane % 2 + half * (HALF * ROWS * 2)
                index = jnp.minimum(index, LANES - 1)
                picked_low = jnp.take_along_axis(low_total, index, axis=1)
                picked_high = jnp.take_along_axis(high_total, index, axis=1)
                edge[half, v] = jnp.where(lane % 4 < 2, picked_high, picked_low)

    def sweep_step(slot, t):
        if slot == 0:
            for copy in chunk_pair(t):
                copy.wait_recv()
            low2, low1, high1, high2 = ([u1[m, k, tile(t)] for m in range(NV)] for k in (0, 1, ROWS + 2, ROWS + 3))
            twelfth = 1.0 / 12.0
            extra = {
                0: mix(0, [twelfth * p - (8.0 * twelfth) * q for p, q in zip(low2, low1)]),
                1: mix(0, [twelfth * q for q in low1]),
                ROWS - 2: mix(0, [-twelfth * q for q in high1]),
                ROWS - 1: mix(0, [(8.0 * twelfth) * q - twelfth * p for p, q in zip(high2, high1)]),
            }
        near = (lane < 2) | (lane >= LANES - 2)
        half = t // HALF
        base = (t % HALF) * ROWS
        ahead = [jnp.zeros((SUB, LANES), F32)] * NV
        start = [jnp.zeros((SUB, LANES), F32)] * NV
        product = jnp.ones((SUB, LANES), F32)
        for i in range(ROWS):
            weight = wgt[i, tile(t)]
            ratio = cc[i, tile(t)]
            for v in range(NV):
                flux = yy[v, i, tile(t)]
                if slot == 0 and i in extra:
                    flux = flux + extra[i][v]
                side = pltpu.roll(edge[half, v], LANES - 2 - 4 * (base + i), 1)
                scaled = weight * (flux + jnp.where(near, side, 0.0))
                if slot == 0 and i == 0:
                    qrow[0, v, tile(t)] = scaled
                if slot == 0 and i == ROWS - 1:
                    qrow[1, v, tile(t)] = scaled
                ahead[v] = (scaled + ahead[v]) * ratio
                yy[v, i, tile(t)] = ahead[v]
                start[v] = start[v] + product * ahead[v]
            product = cp[i, tile(t)]
        for v in range(NV):
            pb[slot, t, v, 0] = start[v]
            pb[slot, t, v, 1] = ahead[v]

    def factor_step(t, carry):
        ratio = jnp.zeros((SUB, LANES), F32)
        product = jnp.ones((SUB, LANES), F32)
        first = jnp.zeros((SUB, LANES), F32)
        for i in range(ROWS):
            inverse = inverse_smoothing(rad[i + 1, tile(t)])
            wgt[i, tile(t)] = -vol[i, tile(t)] * inverse
            ratio = 1.0 / (2.0 + inverse - ratio)
            cc[i, tile(t)] = ratio
            previous = product
            product = product * ratio
            cp[i, tile(t)] = product
            first = first + previous * product
        gg[t, 0] = first
        gg[t, 1] = product
        gg[t, 2] = ratio
        return carry

    lax.fori_loop(0, TILES, factor_step, 0)
    g_pair = begin([remote(gg.at[pl.ds(other, HALF)], gr, gp_s, gp_r, partner)])
    lax.fori_loop(0, TILES, functools.partial(local_step, u1, 0), 0)

    def by_core(own, theirs):
        return jnp.where(core0, own, theirs), jnp.where(core0, theirs, own)

    def join(a_first, a_cross, a_last, b_first, b_cross, b_last):
        d = 1.0 / (1.0 - a_last * b_first)
        return (
            d,
            a_first + a_cross * a_cross * d * b_first,
            a_cross * d * b_cross,
            b_last + b_cross * b_cross * d * a_last,
        )

    def inner_pair(alpha, beta, a_last, b_first, d):
        return d * (alpha + a_last * beta), d * (beta + b_first * alpha)

    g_pair[0].wait_recv()

    def merge_step(t, carry):
        pairs = [by_core(gg[mine + t, n], gr[t, n]) for n in range(3)]
        (a_first, b_first), (a_cross, b_cross), (a_last, b_last) = pairs
        d, first, cross, last = join(a_first, a_cross, a_last, b_first, b_cross, b_last)
        for n, value in enumerate((a_cross, a_last, b_first, b_cross, d)):
            gm[1, t, n] = value
        for n, value in enumerate((first, cross, last)):
            gm[0, t, n] = value
        return carry

    lax.fori_loop(0, HALF, merge_step, 0)

    def unit_send(src_of, dst, ssem, rsem, target):
        return remote(src_of(target), dst.at[me], ssem.at[target], rsem.at[me], rank_device(target))

    def spread(src_of, dst, ssem, rsem, targets):
        for target in targets:

            @pl.when(target != me)
            def _(target=target):
                unit_send(src_of, dst, ssem, rsem, target).start()

    def spread_end(src_of, dst, ssem, rsem):
        for target in range(UNITS):

            @pl.when(target != me)
            def _(target=target):
                unit_send(src_of, dst, ssem, rsem, target).wait_send()

    def spread_recv(dst, rsem):
        for n in range(len(offsets)):
            origin = source(n)
            remote(dst.at[origin], dst.at[origin], rsem.at[origin], rsem.at[origin], rank_device(origin)).wait_recv()

    def g_source(target):
        return gm.at[0, target // NV, pl.ds(0, 3)]

    spread(g_source, gt, ga_s, ga_r, range(UNITS))
    for copy in loads["dt"]:
        copy.wait()
    rad_halo = begin(circ_pair(rad, 0, 1, 1))
    dt_halo = begin(circ_pair(dt, 1, 2, 2))

    def tree_factors():
        for r in range(ranks):
            for n in range(3):
                td[r, n] = gt[r, n]
        first, width, node = 0, ranks, ranks
        while width > 1:
            for k in range(0, width, 2):
                left_node, right_node = first + k, first + k + 1
                d, g0, g1, g2 = join(*(td[left_node, n] for n in range(3)), *(td[right_node, n] for n in range(3)))
                for n, value in enumerate((g0, g1, g2, d)):
                    td[node, n] = value
                node += 1
            first, width = first + width, width // 2
        top = 2 * ranks - 2
        inner = 1.0 - td[top, 1]
        td[top + 1, 0] = 1.0 / (inner * inner - td[top, 0] * td[top, 2])

    def tree_solve(slot):
        levels = []
        first, width, node = 0, ranks, ranks
        for r in range(ranks):
            for n in range(2):
                tp[r, n] = rb[slot, r, n]
        while width > 1:
            for k in range(0, width, 2):
                ln, rn = first + k, first + k + 1
                a0, b0 = inner_pair(tp[ln, 1], tp[rn, 0], td[ln, 2], td[rn, 0], td[node, 3])
                tp[node, 0] = tp[ln, 0] + td[ln, 1] * b0
                tp[node, 1] = tp[rn, 1] + td[rn, 1] * a0
                levels.append((node, ln, rn))
                node += 1
            first, width = first + width, width // 2
        top = 2 * ranks - 2
        inner = 1.0 - td[top, 1]
        det = td[top + 1, 0]
        tx[top, 0] = (inner * tp[top, 1] + td[top, 2] * tp[top, 0]) * det
        tx[top, 1] = (inner * tp[top, 0] + td[top, 0] * tp[top, 1]) * det
        for node, ln, rn in levels[::-1]:
            xl, xh = tx[node, 0], tx[node, 1]
            alpha = tp[ln, 1] + td[ln, 1] * xl
            beta = tp[rn, 0] + td[rn, 1] * xh
            mid_a, mid_b = inner_pair(alpha, beta, td[ln, 2], td[rn, 0], td[node, 3])
            tx[ln, 0] = xl
            tx[ln, 1] = mid_b
            tx[rn, 0] = mid_a
            tx[rn, 1] = xh
        for r in range(ranks):
            for n in range(2):
                xb[slot, r, n] = tx[r, n]

    def pair_copy(slot, step):
        return remote(
            pb.at[slot, other + step], pr.at[slot, step], pp_s.at[slot, step], pp_r.at[slot, step], partner
        )

    def back_copy(slot, step):
        return remote(
            res.at[slot, step], xx.at[slot, mine + step], xp_s.at[slot, step], xp_r.at[slot, step], partner
        )

    def arrival(slot, step):
        return remote(
            res.at[slot, step], xx.at[slot, other + step], xp_s.at[slot, step], xp_r.at[slot, step], partner
        )

    def section(slot):
        edge_fluxes(slot)

        def theirs(step, carry):
            sweep_step(slot, other + step)
            pair_copy(slot, step).start()
            return carry

        lax.fori_loop(0, HALF, theirs, 0)

        def ours(step, carry):
            sweep_step(slot, mine + step)
            pair_copy(slot, step).wait_recv()
            a_cross, a_last, b_first, b_cross, d = (gm[1, step, n] for n in range(5))
            for v in range(NV):
                a_head, b_head = by_core(pb[slot, mine + step, v, 0], pr[slot, step, v, 0])
                a_tail, b_tail = by_core(pb[slot, mine + step, v, 1], pr[slot, step, v, 1])
                a0, b0 = inner_pair(a_tail, b_head, a_last, b_first, d)
                mb[slot, step * NV + v, 0] = a_head + a_cross * b0
                mb[slot, step * NV + v, 1] = b_tail + b_cross * a0
            spread(
                lambda target: mb.at[slot, target],
                rb.at[slot],
                pa_s.at[slot],
                pa_r.at[slot],
                [step * NV + v for v in range(NV)],
            )
            return carry

        lax.fori_loop(0, HALF, ours, 0)

        q_halo = []
        if slot == 0:
            q_halo = begin(
                [
                    remote(qrow.at[0], qhalo.at[1], q_s.at[0], q_r.at[0], left),
                    remote(qrow.at[1], qhalo.at[0], q_s.at[1], q_r.at[1], right),
                ]
            )

        @pl.when(me < UNITS)
        def _():
            if slot == 0:
                gt[me] = gm[0, me // NV, pl.ds(0, 3)]
                spread_recv(gt, ga_r)
                tree_factors()
            rb[slot, me] = mb[slot, me]
            spread_recv(rb.at[slot], pa_r.at[slot])
            tree_solve(slot)
            xr[slot, me] = xb[slot, me]
            for n in range(len(offsets)):
                remote(
                    xb.at[slot, peer(n)], xr.at[slot, me], xa_s.at[slot, n], xa_r.at[slot, me], rank_device(peer(n))
                ).start()

        def unmerge(step, carry):
            for v in range(NV):
                origin = step * NV + v

                @pl.when(origin != me)
                def _(origin=origin):
                    remote(
                        xr.at[slot, origin],
                        xr.at[slot, origin],
                        xa_r.at[slot, origin],
                        xa_r.at[slot, origin],
                        rank_device(origin),
                    ).wait_recv()

            a_cross, a_last, b_first, b_cross, d = (gm[1, step, n] for n in range(5))
            for v in range(NV):
                xl, xh = xr[slot, step * NV + v, 0], xr[slot, step * NV + v, 1]
                _, b_head = by_core(pb[slot, mine + step, v, 0], pr[slot, step, v, 0])
                a_tail, _ = by_core(pb[slot, mine + step, v, 1], pr[slot, step, v, 1])
                mid_a, mid_b = inner_pair(a_tail + a_cross * xl, b_head + b_cross * xh, a_last, b_first, d)
                xx[slot, mine + step, v, 0] = jnp.where(core0, xl, mid_a)
                xx[slot, mine + step, v, 1] = jnp.where(core0, mid_b, xh)
                res[slot, step, v, 0] = jnp.where(core0, mid_a, xl)
                res[slot, step, v, 1] = jnp.where(core0, xh, mid_b)
            back_copy(slot, step).start()
            return carry

        lax.fori_loop(0, HALF, unmerge, 0)
        return q_halo

    def sweep(slot, t, v):
        low, high = xx[slot, t, v, 0], xx[slot, t, v, 1]
        values = [None] * ROWS
        later = high
        for i in range(ROWS - 1, -1, -1):
            later = yy[v, i, tile(t)] + cp[i, tile(t)] * low + cc[i, tile(t)] * later
            values[i] = later
        return low, high, values

    for copy in ax_halo:
        copy.wait_recv()
    q_halo = section(0)
    for copy in q_halo + rad_halo + dt_halo:
        copy.wait_recv()

    def update_one(t, carry):
        diag_low = 2.0 + inverse_smoothing(rad[0, tile(t)])
        diag_high = 2.0 + inverse_smoothing(rad[ROWS + 1, tile(t)])
        for v in range(NV):
            low, high, values = sweep(0, t, v)
            low2 = diag_low * low - values[0] - qhalo[0, v, tile(t)]
            high2 = diag_high * high - values[ROWS - 1] - qhalo[1, v, tile(t)]
            for i, value in enumerate([low2, low] + values + [high, high2]):
                u2[v, i, tile(t)] = u1[v, i, tile(t)] + SECTION_ONE * dt[i, tile(t)] * value
        return pack(u2, t, carry)

    def update_one_late(step, carry):
        arrival(0, step).wait_recv()
        return update_one(other + step, carry)

    packed = lax.fori_loop(0, HALF, lambda step, carry: update_one(mine + step, carry), blank)
    packed = lax.fori_loop(0, HALF, update_one_late, packed)
    keep_packed(1, packed)
    ax_halo = begin(axial_pair(1))
    lax.fori_loop(0, TILES, functools.partial(local_step, u2, 1), 0)
    for copy in ax_halo:
        copy.wait_recv()
    section(1)

    def stores(t):
        return [
            pltpu.make_async_copy(u2.at[:, i + 2, tile(t)], out.at[:, tile(t), i, :], out_sem.at[t, i])
            for i in range(ROWS)
        ]

    def update_two(t, carry):
        for v in range(NV):
            _, _, values = sweep(1, t, v)
            for i, value in enumerate(values):
                u2[v, i + 2, tile(t)] = u1[v, i + 2, tile(t)] + dt[i + 2, tile(t)] * value
        for copy in stores(t):
            copy.start()
        return carry

    def update_two_late(step, carry):
        arrival(1, step).wait_recv()
        return update_two(other + step, carry)

    lax.fori_loop(0, HALF, lambda step, carry: update_two(mine + step, carry), 0)
    lax.fori_loop(0, HALF, update_two_late, 0)

    for copy in pending:
        copy.wait_send()
    spread_end(g_source, gt, ga_s, ga_r)

    def sent(t, carry):
        for copy in chunk_pair(t):
            copy.wait_send()
        return carry

    lax.fori_loop(0, TILES, sent, 0)
    for slot in range(2):
        spread_end(lambda target, slot=slot: mb.at[slot, target], rb.at[slot], pa_s.at[slot], pa_r.at[slot])
        for step in range(HALF):
            pair_copy(slot, step).wait_send()
            back_copy(slot, step).wait_send()

        @pl.when(me < UNITS)
        def _(slot=slot):
            for n in range(len(offsets)):
                remote(
                    xb.at[slot, peer(n)], xr.at[slot, me], xa_s.at[slot, n], xa_r.at[slot, me], rank_device(peer(n))
                ).wait_send()

    def stored(t, carry):
        for copy in stores(t):
            copy.wait()
        return carry

    lax.fori_loop(0, TILES, stored, 0)


def solution(mesh):
    count = mesh.shape["blk"]
    nz, na = count // 4, mesh.shape["axial"]
    split = Mesh(mesh.devices.reshape(nz, 2, 2, na), (*BLK, "axial"))
    ranks = nz * 2

    def on_device(fields, inv_volume, radius_ratio, time_step, jac_circ, jac_other):
        layers = fields.shape[1]
        vmem = lambda *shape: pltpu.VMEM(shape, F32)
        dma = lambda *shape: pltpu.SemaphoreType.DMA(shape)
        plane = (layers, LANES)
        cell = (SUB, LANES)
        peers = ranks - 1
        scratch = [
            vmem(NV, ROWS + 4, *plane),
            vmem(NV, ROWS + 4, *plane),
            vmem(ROWS, *plane),
            vmem(ROWS + 2, *plane),
            vmem(ROWS + 4, *plane),
            vmem(ROWS, *plane),
            vmem(ROWS, *plane),
            vmem(ROWS, *plane),
            vmem(NV, ROWS, *plane),
            vmem(2, NV, *plane),
            vmem(2, NV, *plane),
            vmem(2, 2, NV, *cell),
            vmem(2, 2, NV, *cell),
            vmem(2, TILES, NV, 2, *cell),
            vmem(2, HALF, NV, 2, *cell),
            vmem(2, UNITS, 2, *cell),
            vmem(2, ranks, 2, *cell),
            vmem(2, ranks, 2, *cell),
            vmem(2, UNITS, 2, *cell),
            vmem(2, TILES, NV, 2, *cell),
            vmem(TILES, 3, *cell),
            vmem(HALF, 3, *cell),
            vmem(2, HALF, 5, *cell),
            vmem(ranks, 3, *cell),
            vmem(2 * ranks, 4, *cell),
            vmem(2 * ranks, 2, *cell),
            vmem(2 * ranks, 2, *cell),
            vmem(2, HALF, NV, 2, *cell),
            vmem(3, NV, NV, *cell),
            vmem(2, NV, *cell),
            dma(4, ROWS),
            dma(TILES, ROWS),
            dma(2, TILES),
            dma(2, TILES),
            dma(2, 2),
            dma(2, 2),
            dma(2, 2),
            dma(2, 2),
            dma(2),
            dma(2),
            pltpu.SemaphoreType.DMA,
            pltpu.SemaphoreType.DMA,
            dma(UNITS),
            dma(ranks),
            dma(2, HALF),
            dma(2, HALF),
            dma(2, UNITS),
            dma(2, ranks),
            dma(2, peers),
            dma(2, ranks),
            dma(2, HALF),
            dma(2, HALF),
        ]
        anywhere = pl.BlockSpec(memory_space=pl.ANY)
        scalars = pl.BlockSpec(memory_space=pltpu.SMEM)
        return pl.pallas_call(
            functools.partial(kernel, nz, na),
            out_shape=jax.ShapeDtypeStruct(fields.shape, F32),
            in_specs=[anywhere] * 4 + [scalars] * 2,
            out_specs=anywhere,
            scratch_shapes=scratch,
            compiler_params=pltpu.CompilerParams(collective_id=0, has_side_effects=True),
        )(fields, inv_volume, radius_ratio, time_step, jac_circ, jnp.transpose(jac_other, (1, 0, 2)))

    return jax.shard_map(
        on_device,
        mesh=split,
        in_specs=(
            P(None, None, BLK, "axial"),
            P(None, BLK, "axial"),
            P(None, BLK, "axial"),
            P(None, BLK, "axial"),
            P(),
            P(),
        ),
        out_specs=P(None, None, BLK, "axial"),
        check_vma=False,
    )
```

```python
import functools

import jax
import jax.numpy as jnp
from jax import lax
from jax.experimental import pallas as pl
from jax.experimental.pallas import tpu as pltpu
from jax.sharding import Mesh
from jax.sharding import PartitionSpec as P

BLK = ("blk_0", "blk_1", "blk_2")
DISSIPATION = 0.03125
SECTION_ONE = 0.6
COURANT_RATIO = 2.0
SCALING_POWER = 2.0 / 3.0

NV = 5
TILES = 6
HALF = 3
ROWS = 8
SUB = 8
SPLIT = 2
LANES = 128
UNITS = HALF * NV
F32 = jnp.float32


def kernel(
    nz,
    na,
    fields,
    inv_volume,
    radius_ratio,
    time_step,
    jac_c,
    jac_o,
    out,
    u1,
    u2,
    vol,
    rad,
    dt,
    wgt,
    cc,
    cp,
    yy,
    qrow,
    qhalo,
    pk,
    pkh,
    pb,
    pr,
    mb,
    rb,
    xb,
    xr,
    xx,
    gg,
    gr,
    gm,
    gt,
    td,
    tp,
    tx,
    res,
    tab,
    edge,
    in_sem,
    out_sem,
    uc_s,
    uc_r,
    circ_s,
    circ_r,
    ax_s,
    ax_r,
    q_s,
    q_r,
    gp_s,
    gp_r,
    ga_s,
    ga_r,
    pp_s,
    pp_r,
    pa_s,
    pa_r,
    xa_s,
    xa_r,
    xp_s,
    xp_r,
    ready,
):
    ranks = nz * 2
    z = lax.axis_index("blk_0")
    y = lax.axis_index("blk_1")
    c = lax.axis_index("blk_2")
    a = lax.axis_index("axial")
    me = z * 2 + y

    def blk_device(b):
        return {"blk_0": b // 4, "blk_1": (b // 2) % 2, "blk_2": b % 2, "axial": a}

    def ax_device(index):
        return {"blk_0": z, "blk_1": y, "blk_2": c, "axial": index}

    def rank_device(rank):
        return {"blk_0": rank // 2, "blk_1": rank % 2, "blk_2": c, "axial": a}

    b = me * 2 + c
    size = ranks * 2
    right = blk_device((b + 1) % size)
    left = blk_device((b + size - 1) % size)
    ax_up = ax_device((a + 1) % na)
    ax_down = ax_device((a + na - 1) % na)
    partner = {"blk_0": z, "blk_1": y, "blk_2": 1 - c, "axial": a}
    hops = [dz for k in range(nz // 2, 0, -1) for dz in dict.fromkeys((k, nz - k))] + [0]
    offsets = [(dz, dy) for dz in hops for dy in (1, 0) if (dz, dy) != (0, 0)]

    def peer(n):
        dz, dy = offsets[n]
        return ((z + dz) % nz) * 2 + (y + dy) % 2

    def source(n):
        dz, dy = offsets[n]
        return ((z + nz - dz) % nz) * 2 + (y + dy) % 2

    def remote(src, dst, ssem, rsem, device):
        return pltpu.make_async_remote_copy(
            src_ref=src,
            dst_ref=dst,
            send_sem=ssem,
            recv_sem=rsem,
            device_id=device,
            device_id_type=pl.DeviceIdType.MESH,
        )

    def load_u(i, group):
        pltpu.make_async_copy(fields.at[:, :, i, :], u1.at[:, i + 2], in_sem.at[group]).start()

    def load_cell(source_ref, target_ref, shift, group):
        for i in range(ROWS):
            pltpu.make_async_copy(source_ref.at[:, i, :], target_ref.at[i + shift], in_sem.at[group]).start()

    def landed(part, semaphore):
        pltpu.make_async_copy(part, part, semaphore).wait()

    def beside(dz, dy):
        return rank_device(((z + nz + dz) % nz) * 2 + (y + dy) % 2)

    def signal(semaphore, device):
        pl.semaphore_signal(semaphore, inc=1, device_id=device, device_id_type=pl.DeviceIdType.MESH)

    barrier = pltpu.get_barrier_semaphore()
    greet = [ax_up, ax_down, right, left, beside(1, 1), beside(-1, 1), beside(1, 0), beside(-1, 0), beside(0, 1), partner]
    edge_rows, inner_rows = (0, 1, ROWS - 2, ROWS - 1), range(2, ROWS - 2)
    for i in edge_rows:
        load_u(i, 0)
    for device in greet:
        signal(barrier, device)
    for i in inner_rows:
        load_u(i, 1)

    def ready_signal(n):
        for dz in (1, -1):
            signal(ready.at[n], beside(dz, 0))

    def ready_wait(n):
        pl.semaphore_wait(ready.at[n], 2)

    lane = lax.broadcasted_iota(jnp.int32, (SUB, LANES), 1)
    sub = lax.broadcasted_iota(jnp.int32, (SUB, LANES), 0)
    core0 = jnp.broadcast_to(c == 0, (SUB, LANES))

    def tile(t):
        return pl.ds(pl.multiple_of(t * SUB, SUB), SUB)

    def inverse_smoothing(ratio):
        scaled = COURANT_RATIO * (1.0 + jnp.exp(SCALING_POWER * jnp.log(ratio)))
        return 1.0 / (0.25 * (scaled * scaled - 1.0))

    def pack(u, t, carry):
        packed = list(carry)
        group = lane // 2 - t * ROWS
        for v in range(NV):
            for i in range(ROWS):
                moved = pltpu.roll(u[v, i + 2, tile(t)], 2 * (t * ROWS + i) + 2, 1)
                packed[v] = jnp.where(group == i, moved, packed[v])
                packed[NV + v] = jnp.where(group == i + 1, moved, packed[NV + v])
        return tuple(packed)

    def keep_packed(slot, packed):
        for v in range(NV):
            pk[slot, 0, v] = packed[v]
            pk[slot, 1, v] = packed[NV + v]

    blank = (jnp.zeros((SUB, LANES), F32),) * (2 * NV)

    landed(u1.at[:, pl.ds(2, len(edge_rows))], in_sem.at[0])
    pl.semaphore_wait(barrier, len(greet))

    def circ_pair(ref, which, low, width):
        def part(start):
            return ref.at[pl.ds(start, width)]

        count = ROWS
        to_left = remote(part(low), part(low + count), circ_s.at[which, 0], circ_r.at[which, 0], left)
        to_right = remote(part(low + count - width), part(low - width), circ_s.at[which, 1], circ_r.at[which, 1], right)
        return [to_left, to_right]

    def axial_pair(slot):
        up = remote(pk.at[slot, 0], pkh.at[slot, 0], ax_s.at[slot, 0], ax_r.at[slot, 0], ax_up)
        down = remote(pk.at[slot, 1], pkh.at[slot, 1], ax_s.at[slot, 1], ax_r.at[slot, 1], ax_down)
        return [up, down]

    def chunk_pair(t):
        def part(start):
            return u1.at[:, pl.ds(start, 2), tile(t)]

        to_left = remote(part(2), part(ROWS + 2), uc_s.at[0, t], uc_r.at[0, t], left)
        to_right = remote(part(ROWS), part(0), uc_s.at[1, t], uc_r.at[1, t], right)
        return [to_left, to_right]

    pending = []

    def begin(copies):
        for copy in copies:
            copy.start()
        pending.extend(copies)
        return copies

    other = HALF * (1 - c)
    mine = HALF * c

    def chunk_send(step, carry):
        for copy in chunk_pair((step + mine) % TILES):
            copy.start()
        return carry

    lax.fori_loop(0, TILES, chunk_send, 0)
    ready_signal(0)
    load_cell(radius_ratio, rad, 1, 2)
    load_cell(inv_volume, vol, 0, 3)
    landed(u1.at[:, pl.ds(2, len(inner_rows))], in_sem.at[1])
    keep_packed(0, lax.fori_loop(0, TILES, functools.partial(pack, u1), blank))
    ax_halo = begin(axial_pair(0))
    for v in range(NV):
        for m in range(NV):
            tab[0, v, m] = jnp.broadcast_to(jac_c[v, m] / 12.0, (SUB, LANES))
            tab[1, v, m] = jnp.broadcast_to(0.5 * jac_o[v, 0, m], (SUB, LANES))
            tab[2, v, m] = jnp.broadcast_to(0.5 * jac_o[v, 1, m], (SUB, LANES))

    load_cell(time_step, dt, 2, 4)
    landed(rad.at[pl.ds(1, ROWS)], in_sem.at[2])
    landed(vol, in_sem.at[3])

    def splat(value):
        return jnp.broadcast_to(value, (SUB, LANES))

    def local_step(u, slot, t, carry):
        above = jnp.minimum(t * SUB + SUB, TILES * SUB - 1)
        below = jnp.maximum(t * SUB - 1, 0)
        for i in range(ROWS):
            total = [None] * NV
            for m in range(NV):

                def row(k):
                    return u[m, k + 2, tile(t)] if slot == 1 or 0 <= k < ROWS else None

                def minus(p, q):
                    if p is None:
                        return -q
                    return p if q is None else p - q

                centre = u[m, i + 2, tile(t)]
                circ = 8.0 * minus(row(i + 1), row(i - 1)) - minus(row(i + 2), row(i - 2))
                plus1 = pltpu.roll(centre, LANES - 1, 1)
                plus2 = pltpu.roll(centre, LANES - 2, 1)
                minus1 = pltpu.roll(centre, 1, 1)
                minus2 = pltpu.roll(centre, 2, 1)
                axial = plus1 - minus1
                fourth = (plus2 + minus2) - 4.0 * (plus1 + minus1) + 6.0 * centre
                over = jnp.where(
                    sub == SUB - 1, splat(u[m, i + 2, pl.ds(above, 1)]), pltpu.roll(centre, SUB - 1, 0)
                )
                under = jnp.where(sub == 0, splat(u[m, i + 2, pl.ds(below, 1)]), pltpu.roll(centre, 1, 0))
                normal = over - under
                for v in range(NV):
                    term = tab[0, v, m] * circ + tab[1, v, m] * axial + tab[2, v, m] * normal
                    if v == m:
                        term = term + DISSIPATION * fourth
                    total[v] = term if total[v] is None else total[v] + term
            for v in range(NV):
                yy[v, i, tile(t)] = total[v]
        return carry

    def mix(which, values):
        out_values = []
        for v in range(NV):
            total = tab[which, v, 0] * values[0]
            for m in range(1, NV):
                total = total + tab[which, v, m] * values[m]
            out_values.append(total)
        return out_values

    def edge_fluxes(slot):
        even = lane % 2 == 0
        low_edge = jnp.broadcast_to(a == 0, (SUB, LANES))
        high_edge = jnp.broadcast_to(a == na - 1, (SUB, LANES))
        low = [jnp.where(low_edge, 0.0, pkh[slot, 0, v]) - pk[slot, 0, v] for v in range(NV)]
        high = [
            pltpu.roll(jnp.where(high_edge, 0.0, pkh[slot, 1, v]) - pk[slot, 1, v], LANES - 2, 1) for v in range(NV)
        ]
        low_next = [pltpu.roll(value, LANES - 1, 1) for value in low]
        high_next = [pltpu.roll(value, 1, 1) for value in high]
        low_flux = mix(1, [jnp.where(even, -value, 0.0) for value in low_next])
        high_flux = mix(1, [jnp.where(even, 0.0, value) for value in high_next])
        for v in range(NV):
            low_total = low_flux[v] + DISSIPATION * jnp.where(even, low[v] - 4.0 * low_next[v], low[v])
            high_total = high_flux[v] + DISSIPATION * jnp.where(even, high[v], high[v] - 4.0 * high_next[v])
            for half in range(2):
                index = (lane // 4) * 2 + lane % 2 + half * (HALF * ROWS * 2)
                index = jnp.minimum(index, LANES - 1)
                picked_low = jnp.take_along_axis(low_total, index, axis=1)
                picked_high = jnp.take_along_axis(high_total, index, axis=1)
                edge[half, v] = jnp.where(lane % 4 < 2, picked_high, picked_low)

    def sweep_step(slot, t):
        if slot == 0:
            for copy in chunk_pair(t):
                copy.wait_recv()
            low2, low1, high1, high2 = ([u1[m, k, tile(t)] for m in range(NV)] for k in (0, 1, ROWS + 2, ROWS + 3))
            extra = {
                0: mix(0, [p - 8.0 * q for p, q in zip(low2, low1)]),
                1: mix(0, low1),
                ROWS - 2: mix(0, [-q for q in high1]),
                ROWS - 1: mix(0, [8.0 * q - p for p, q in zip(high2, high1)]),
            }
        near = (lane < 2) | (lane >= LANES - 2)
        half = t // HALF
        base = (t % HALF) * ROWS
        ahead = [jnp.zeros((SUB, LANES), F32)] * NV
        start = [jnp.zeros((SUB, LANES), F32)] * NV
        product = jnp.ones((SUB, LANES), F32)
        for i in range(ROWS):
            weight = wgt[i, tile(t)]
            ratio = cc[i, tile(t)]
            for v in range(NV):
                flux = yy[v, i, tile(t)]
                if slot == 0 and i in extra:
                    flux = flux + extra[i][v]
                side = pltpu.roll(edge[half, v], LANES - 2 - 4 * (base + i), 1)
                scaled = weight * (flux + jnp.where(near, side, 0.0))
                if slot == 0 and i == 0:
                    qrow[0, v, tile(t)] = scaled
                if slot == 0 and i == ROWS - 1:
                    qrow[1, v, tile(t)] = scaled
                ahead[v] = (scaled + ahead[v]) * ratio
                yy[v, i, tile(t)] = ahead[v]
                start[v] = start[v] + product * ahead[v]
            product = cp[i, tile(t)]
        for v in range(NV):
            pb[slot, t, v, 0] = start[v]
            pb[slot, t, v, 1] = ahead[v]

    def factor_step(t, carry):
        ratio = jnp.zeros((SUB, LANES), F32)
        product = jnp.ones((SUB, LANES), F32)
        first = jnp.zeros((SUB, LANES), F32)
        for i in range(ROWS):
            inverse = inverse_smoothing(rad[i + 1, tile(t)])
            wgt[i, tile(t)] = -vol[i, tile(t)] * inverse
            ratio = 1.0 / (2.0 + inverse - ratio)
            cc[i, tile(t)] = ratio
            previous = product
            product = product * ratio
            cp[i, tile(t)] = product
            first = first + previous * product
        gg[t, 0] = first
        gg[t, 1] = product
        gg[t, 2] = ratio
        return carry

    lax.fori_loop(0, TILES, factor_step, 0)
    g_pair = begin([remote(gg.at[pl.ds(other, HALF)], gr, gp_s, gp_r, partner)])
    ready_wait(0)
    ready_signal(1)
    lax.fori_loop(0, SPLIT, functools.partial(local_step, u1, 0), 0)
    ready_wait(1)
    ready_signal(2)

    def by_core(own, theirs):
        return jnp.where(core0, own, theirs), jnp.where(core0, theirs, own)

    def join(a_first, a_cross, a_last, b_first, b_cross, b_last):
        d = 1.0 / (1.0 - a_last * b_first)
        return (
            d,
            a_first + a_cross * a_cross * d * b_first,
            a_cross * d * b_cross,
            b_last + b_cross * b_cross * d * a_last,
        )

    def inner_pair(alpha, beta, a_last, b_first, d):
        return d * (alpha + a_last * beta), d * (beta + b_first * alpha)

    g_pair[0].wait_recv()

    def merge_step(t, carry):
        pairs = [by_core(gg[mine + t, n], gr[t, n]) for n in range(3)]
        (a_first, b_first), (a_cross, b_cross), (a_last, b_last) = pairs
        d, first, cross, last = join(a_first, a_cross, a_last, b_first, b_cross, b_last)
        for n, value in enumerate((a_cross, a_last, b_first, b_cross, d)):
            gm[1, t, n] = value
        for n, value in enumerate((first, cross, last)):
            gm[0, t, n] = value
        return carry

    lax.fori_loop(0, HALF, merge_step, 0)

    def spread(src_of, dst, ssem, rsem, targets):
        for target in targets:

            @pl.when(target != me)
            def _(target=target):
                remote(src_of(target), dst.at[me], ssem, rsem, rank_device(target)).start()

    def group_recv(dst, rsem, count):
        part = dst.at[pl.ds(0, count)]
        remote(part, part, rsem, rsem, partner).wait_recv()

    def group_sent(src, ssem, count):
        part = src.at[pl.ds(0, count)]
        remote(part, part, ssem, ssem, partner).wait_send()

    def spread_end(src, ssem):
        @pl.when(me < UNITS)
        def _():
            group_sent(src, ssem, UNITS - 1)

        @pl.when(me >= UNITS)
        def _():
            group_sent(src, ssem, UNITS)

    def g_source(target):
        return gm.at[0, target // NV, pl.ds(0, 3)]

    ready_wait(2)
    spread(g_source, gt, ga_s, ga_r, range(UNITS))
    lax.fori_loop(SPLIT, TILES, functools.partial(local_step, u1, 0), 0)
    landed(dt.at[pl.ds(2, ROWS)], in_sem.at[4])

    def tree_factors():
        for r in range(ranks):
            for n in range(3):
                td[r, n] = gt[r, n]
        first, width, node = 0, ranks, ranks
        while width > 1:
            for k in range(0, width, 2):
                left_node, right_node = first + k, first + k + 1
                d, g0, g1, g2 = join(*(td[left_node, n] for n in range(3)), *(td[right_node, n] for n in range(3)))
                for n, value in enumerate((g0, g1, g2, d)):
                    td[node, n] = value
                node += 1
            first, width = first + width, width // 2
        top = 2 * ranks - 2
        inner = 1.0 - td[top, 1]
        td[top + 1, 0] = 1.0 / (inner * inner - td[top, 0] * td[top, 2])

    def tree_solve(slot):
        levels = []
        first, width, node = 0, ranks, ranks
        for r in range(ranks):
            for n in range(2):
                tp[r, n] = rb[slot, r, n]
        while width > 1:
            for k in range(0, width, 2):
                ln, rn = first + k, first + k + 1
                a0, b0 = inner_pair(tp[ln, 1], tp[rn, 0], td[ln, 2], td[rn, 0], td[node, 3])
                tp[node, 0] = tp[ln, 0] + td[ln, 1] * b0
                tp[node, 1] = tp[rn, 1] + td[rn, 1] * a0
                levels.append((node, ln, rn))
                node += 1
            first, width = first + width, width // 2
        top = 2 * ranks - 2
        inner = 1.0 - td[top, 1]
        det = td[top + 1, 0]
        tx[top, 0] = (inner * tp[top, 1] + td[top, 2] * tp[top, 0]) * det
        tx[top, 1] = (inner * tp[top, 0] + td[top, 0] * tp[top, 1]) * det
        for node, ln, rn in levels[::-1]:
            xl, xh = tx[node, 0], tx[node, 1]
            alpha = tp[ln, 1] + td[ln, 1] * xl
            beta = tp[rn, 0] + td[rn, 1] * xh
            mid_a, mid_b = inner_pair(alpha, beta, td[ln, 2], td[rn, 0], td[node, 3])
            tx[ln, 0] = xl
            tx[ln, 1] = mid_b
            tx[rn, 0] = mid_a
            tx[rn, 1] = xh
        for r in range(ranks):
            for n in range(2):
                xb[slot, r, n] = tx[r, n]

    def pair_copy(slot, step):
        return remote(
            pb.at[slot, other + step], pr.at[slot, step], pp_s.at[slot, step], pp_r.at[slot, step], partner
        )

    def back_copy(slot, step):
        return remote(
            res.at[slot, step], xx.at[slot, mine + step], xp_s.at[slot, step], xp_r.at[slot, step], partner
        )

    def arrival(slot, step):
        return remote(
            res.at[slot, step], xx.at[slot, other + step], xp_s.at[slot, step], xp_r.at[slot, step], partner
        )

    def section_sent(slot):
        spread_end(mb.at[slot], pa_s.at[slot])

        @pl.when(me < UNITS)
        def _():
            group_sent(xb.at[slot], xa_s.at[slot], ranks - 1)

        for step in range(HALF):
            pair_copy(slot, step).wait_send()
            back_copy(slot, step).wait_send()

    def first_sent():
        for copy in pending:
            copy.wait_send()
        pending.clear()
        spread_end(gt, ga_s)

        def sent(t, carry):
            for copy in chunk_pair(t):
                copy.wait_send()
            return carry

        lax.fori_loop(0, TILES, sent, 0)
        section_sent(0)

    def section(slot):
        edge_fluxes(slot)

        def theirs(step, carry):
            sweep_step(slot, other + step)
            pair_copy(slot, step).start()
            return carry

        lax.fori_loop(0, HALF, theirs, 0)

        def ours(step, carry):
            sweep_step(slot, mine + step)
            pair_copy(slot, step).wait_recv()
            a_cross, a_last, b_first, b_cross, d = (gm[1, step, n] for n in range(5))
            for v in range(NV):
                a_head, b_head = by_core(pb[slot, mine + step, v, 0], pr[slot, step, v, 0])
                a_tail, b_tail = by_core(pb[slot, mine + step, v, 1], pr[slot, step, v, 1])
                a0, b0 = inner_pair(a_tail, b_head, a_last, b_first, d)
                mb[slot, step * NV + v, 0] = a_head + a_cross * b0
                mb[slot, step * NV + v, 1] = b_tail + b_cross * a0
            spread(
                lambda target: mb.at[slot, target],
                rb.at[slot],
                pa_s.at[slot],
                pa_r.at[slot],
                [step * NV + v for v in range(NV)],
            )
            return carry

        lax.fori_loop(0, HALF, ours, 0)

        q_halo = []
        if slot == 0:
            q_halo = begin(
                circ_pair(rad, 0, 1, 1)
                + circ_pair(dt, 1, 2, 2)
                + [
                    remote(qrow.at[0], qhalo.at[1], q_s.at[0], q_r.at[0], left),
                    remote(qrow.at[1], qhalo.at[0], q_s.at[1], q_r.at[1], right),
                ]
            )

        if slot == 1:
            first_sent()

        @pl.when(me < UNITS)
        def _():
            if slot == 0:
                gt[me] = gm[0, me // NV, pl.ds(0, 3)]
                group_recv(gt, ga_r, ranks - 1)
                tree_factors()
            rb[slot, me] = mb[slot, me]
            group_recv(rb.at[slot], pa_r.at[slot], ranks - 1)
            tree_solve(slot)
            xr[slot, me] = xb[slot, me]
            for n in range(len(offsets)):
                remote(
                    xb.at[slot, peer(n)], xr.at[slot, me], xa_s.at[slot], xa_r.at[slot, me // NV], rank_device(peer(n))
                ).start()

        def unmerge(step, carry):
            @pl.when(me // NV == step)
            def _():
                group_recv(xr.at[slot], xa_r.at[slot, step], NV - 1)

            @pl.when(me // NV != step)
            def _():
                group_recv(xr.at[slot], xa_r.at[slot, step], NV)

            a_cross, a_last, b_first, b_cross, d = (gm[1, step, n] for n in range(5))
            for v in range(NV):
                xl, xh = xr[slot, step * NV + v, 0], xr[slot, step * NV + v, 1]
                _, b_head = by_core(pb[slot, mine + step, v, 0], pr[slot, step, v, 0])
                a_tail, _ = by_core(pb[slot, mine + step, v, 1], pr[slot, step, v, 1])
                mid_a, mid_b = inner_pair(a_tail + a_cross * xl, b_head + b_cross * xh, a_last, b_first, d)
                xx[slot, mine + step, v, 0] = jnp.where(core0, xl, mid_a)
                xx[slot, mine + step, v, 1] = jnp.where(core0, mid_b, xh)
                res[slot, step, v, 0] = jnp.where(core0, mid_a, xl)
                res[slot, step, v, 1] = jnp.where(core0, xh, mid_b)
            back_copy(slot, step).start()
            return carry

        lax.fori_loop(0, HALF, unmerge, 0)
        return q_halo

    def sweep(slot, t, v):
        low, high = xx[slot, t, v, 0], xx[slot, t, v, 1]
        values = [None] * ROWS
        later = high
        for i in range(ROWS - 1, -1, -1):
            later = yy[v, i, tile(t)] + cp[i, tile(t)] * low + cc[i, tile(t)] * later
            values[i] = later
        return low, high, values

    for copy in ax_halo:
        copy.wait_recv()
    q_halo = section(0)
    for copy in q_halo:
        copy.wait_recv()

    def update_one(t, carry):
        diag_low = 2.0 + inverse_smoothing(rad[0, tile(t)])
        diag_high = 2.0 + inverse_smoothing(rad[ROWS + 1, tile(t)])
        for v in range(NV):
            low, high, values = sweep(0, t, v)
            low2 = diag_low * low - values[0] - qhalo[0, v, tile(t)]
            high2 = diag_high * high - values[ROWS - 1] - qhalo[1, v, tile(t)]
            for i, value in enumerate([low2, low] + values + [high, high2]):
                u2[v, i, tile(t)] = u1[v, i, tile(t)] + SECTION_ONE * dt[i, tile(t)] * value
        return pack(u2, t, carry)

    def update_one_late(step, carry):
        arrival(0, step).wait_recv()
        return update_one(other + step, carry)

    packed = lax.fori_loop(0, HALF, lambda step, carry: update_one(mine + step, carry), blank)
    packed = lax.fori_loop(0, HALF, update_one_late, packed)
    keep_packed(1, packed)
    ax_halo = begin(axial_pair(1))
    lax.fori_loop(0, TILES, functools.partial(local_step, u2, 1), 0)
    for copy in ax_halo:
        copy.wait_recv()
    section(1)

    def stores(t):
        return [
            pltpu.make_async_copy(u2.at[:, i + 2, tile(t)], out.at[:, tile(t), i, :], out_sem)
            for i in range(ROWS)
        ]

    def update_two(t, carry):
        for v in range(NV):
            _, _, values = sweep(1, t, v)
            for i, value in enumerate(values):
                u2[v, i + 2, tile(t)] = u1[v, i + 2, tile(t)] + dt[i + 2, tile(t)] * value
        for copy in stores(t):
            copy.start()
        return carry

    def update_two_late(step, carry):
        arrival(1, step).wait_recv()
        return update_two(other + step, carry)

    lax.fori_loop(0, HALF, lambda step, carry: update_two(mine + step, carry), 0)
    lax.fori_loop(0, HALF, update_two_late, 0)
    section_sent(1)

    landed(u2.at[:, pl.ds(2, ROWS)], out_sem)


def solution(mesh):
    count = mesh.shape["blk"]
    nz, na = count // 4, mesh.shape["axial"]
    split = Mesh(mesh.devices.reshape(nz, 2, 2, na), (*BLK, "axial"))
    ranks = nz * 2

    def on_device(fields, inv_volume, radius_ratio, time_step, jac_circ, jac_other):
        layers = fields.shape[1]
        vmem = lambda *shape: pltpu.VMEM(shape, F32)
        dma = lambda *shape: pltpu.SemaphoreType.DMA(shape)
        plane = (layers, LANES)
        cell = (SUB, LANES)
        scratch = [
            vmem(NV, ROWS + 4, *plane),
            vmem(NV, ROWS + 4, *plane),
            vmem(ROWS, *plane),
            vmem(ROWS + 2, *plane),
            vmem(ROWS + 4, *plane),
            vmem(ROWS, *plane),
            vmem(ROWS, *plane),
            vmem(ROWS, *plane),
            vmem(NV, ROWS, *plane),
            vmem(2, NV, *plane),
            vmem(2, NV, *plane),
            vmem(2, 2, NV, *cell),
            vmem(2, 2, NV, *cell),
            vmem(2, TILES, NV, 2, *cell),
            vmem(2, HALF, NV, 2, *cell),
            vmem(2, UNITS, 2, *cell),
            vmem(2, ranks, 2, *cell),
            vmem(2, ranks, 2, *cell),
            vmem(2, UNITS, 2, *cell),
            vmem(2, TILES, NV, 2, *cell),
            vmem(TILES, 3, *cell),
            vmem(HALF, 3, *cell),
            vmem(2, HALF, 5, *cell),
            vmem(ranks, 3, *cell),
            vmem(2 * ranks, 4, *cell),
            vmem(2 * ranks, 2, *cell),
            vmem(2 * ranks, 2, *cell),
            vmem(2, HALF, NV, 2, *cell),
            vmem(3, NV, NV, *cell),
            vmem(2, NV, *cell),
            dma(5),
            pltpu.SemaphoreType.DMA,
            dma(2, TILES),
            dma(2, TILES),
            dma(2, 2),
            dma(2, 2),
            dma(2, 2),
            dma(2, 2),
            dma(2),
            dma(2),
            pltpu.SemaphoreType.DMA,
            pltpu.SemaphoreType.DMA,
            pltpu.SemaphoreType.DMA,
            pltpu.SemaphoreType.DMA,
            dma(2, HALF),
            dma(2, HALF),
            dma(2),
            dma(2),
            dma(2),
            dma(2, HALF),
            dma(2, HALF),
            dma(2, HALF),
            pltpu.SemaphoreType.REGULAR((3,)),
        ]
        anywhere = pl.BlockSpec(memory_space=pl.ANY)
        scalars = pl.BlockSpec(memory_space=pltpu.SMEM)
        return pl.pallas_call(
            functools.partial(kernel, nz, na),
            out_shape=jax.ShapeDtypeStruct(fields.shape, F32),
            in_specs=[anywhere] * 4 + [scalars] * 2,
            out_specs=anywhere,
            scratch_shapes=scratch,
            compiler_params=pltpu.CompilerParams(collective_id=0, has_side_effects=True),
        )(fields, inv_volume, radius_ratio, time_step, jac_circ, jnp.transpose(jac_other, (1, 0, 2)))

    return jax.shard_map(
        on_device,
        mesh=split,
        in_specs=(
            P(None, None, BLK, "axial"),
            P(None, BLK, "axial"),
            P(None, BLK, "axial"),
            P(None, BLK, "axial"),
            P(),
            P(),
        ),
        out_specs=P(None, None, BLK, "axial"),
        check_vma=False,
    )
```

```python
import functools

import jax
import jax.numpy as jnp
from jax import lax
from jax.experimental import pallas as pl
from jax.experimental.pallas import tpu as pltpu
from jax.sharding import Mesh
from jax.sharding import PartitionSpec as P

BLK = ("blk_0", "blk_1", "blk_2")
DISSIPATION = 0.03125
SECTION_ONE = 0.6
COURANT_RATIO = 2.0
SCALING_POWER = 2.0 / 3.0

NV = 5
TILES = 6
HALF = 3
ROWS = 8
SUB = 8
SPLIT = 2
LANES = 128
UNITS = HALF * NV
F32 = jnp.float32


def kernel(
    nz,
    na,
    fields,
    inv_volume,
    radius_ratio,
    time_step,
    jac_c,
    jac_o,
    out,
    u1,
    u2,
    vol,
    rad,
    dt,
    wgt,
    cc,
    cp,
    yy,
    qrow,
    qhalo,
    pk,
    pkh,
    pb,
    pr,
    mb,
    rb,
    xb,
    xr,
    xx,
    gg,
    gr,
    gm,
    gt,
    td,
    tp,
    tx,
    res,
    tab,
    edge,
    in_sem,
    uc_s,
    uc_r,
    circ_s,
    circ_r,
    ax_s,
    ax_r,
    q_s,
    q_r,
    gp_s,
    gp_r,
    ga_s,
    ga_r,
    pp_s,
    pp_r,
    pa_s,
    pa_r,
    xa_s,
    xa_r,
    xp_s,
    xp_r,
    ready,
):
    ranks = nz * 2
    z = lax.axis_index("blk_0")
    y = lax.axis_index("blk_1")
    c = lax.axis_index("blk_2")
    a = lax.axis_index("axial")
    me = z * 2 + y

    def blk_device(b):
        return {"blk_0": lax.div(b, 4), "blk_1": lax.rem(lax.div(b, 2), 2), "blk_2": lax.rem(b, 2), "axial": a}

    def ax_device(index):
        return {"blk_0": z, "blk_1": y, "blk_2": c, "axial": index}

    def rank_device(rank):
        if isinstance(rank, int):
            return {"blk_0": rank // 2, "blk_1": rank % 2, "blk_2": c, "axial": a}
        return {"blk_0": lax.div(rank, 2), "blk_1": lax.rem(rank, 2), "blk_2": c, "axial": a}

    def plane_device(plane, column):
        return {"blk_0": plane, "blk_1": column, "blk_2": c, "axial": a}

    def around(value, count):
        return lax.rem(value, count)

    b = me * 2 + c
    size = ranks * 2
    right = blk_device(around(b + 1, size))
    left = blk_device(around(b + size - 1, size))
    ax_up = ax_device(around(a + 1, na))
    ax_down = ax_device(around(a + na - 1, na))
    partner = {"blk_0": z, "blk_1": y, "blk_2": 1 - c, "axial": a}
    hops = [dz for k in range(nz // 2, 0, -1) for dz in dict.fromkeys((k, nz - k))] + [0]
    offsets = [(dz, dy) for dz in hops for dy in (1, 0) if (dz, dy) != (0, 0)]

    def peer(n):
        dz, dy = offsets[n]
        return around(z + dz, nz), (1 - y if dy else y)

    def remote(src, dst, ssem, rsem, device):
        return pltpu.make_async_remote_copy(
            src_ref=src,
            dst_ref=dst,
            send_sem=ssem,
            recv_sem=rsem,
            device_id=device,
            device_id_type=pl.DeviceIdType.MESH,
        )

    def load_u(i, group):
        pltpu.make_async_copy(fields.at[:, :, i, :], u1.at[:, i + 2], in_sem.at[group]).start()

    def load_cell(source_ref, target_ref, shift, group):
        for i in range(ROWS):
            pltpu.make_async_copy(source_ref.at[:, i, :], target_ref.at[i + shift], in_sem.at[group]).start()

    def landed(part, semaphore):
        pltpu.make_async_copy(part, part, semaphore).wait()

    def beside(dz, dy):
        return plane_device(around(z + nz + dz, nz), 1 - y if dy else y)

    def signal(semaphore, device):
        pl.semaphore_signal(semaphore, inc=1, device_id=device, device_id_type=pl.DeviceIdType.MESH)

    barrier = pltpu.get_barrier_semaphore()
    greet = [ax_up, ax_down, right, left, beside(1, 1), beside(-1, 1), beside(1, 0), beside(-1, 0), beside(0, 1), partner]
    edge_rows, inner_rows = (0, 1, ROWS - 2, ROWS - 1), range(2, ROWS - 2)
    for i in edge_rows:
        load_u(i, 0)
    for device in greet:
        signal(barrier, device)
    for i in inner_rows:
        load_u(i, 1)

    def ready_signal(n):
        for dz in (1, -1):
            signal(ready.at[n], beside(dz, 0))

    def ready_wait(n):
        pl.semaphore_wait(ready.at[n], 2)

    lane = lax.broadcasted_iota(jnp.int32, (SUB, LANES), 1)
    sub = lax.broadcasted_iota(jnp.int32, (SUB, LANES), 0)
    core0 = jnp.broadcast_to(c == 0, (SUB, LANES))

    def tile(t):
        return pl.ds(pl.multiple_of(t * SUB, SUB), SUB)

    def inverse_smoothing(ratio):
        scaled = COURANT_RATIO * (1.0 + jnp.exp(SCALING_POWER * jnp.log(ratio)))
        return 1.0 / (0.25 * (scaled * scaled - 1.0))

    def pack(u, t, carry):
        packed = list(carry)
        group = lane // 2 - t * ROWS
        for v in range(NV):
            for i in range(ROWS):
                moved = pltpu.roll(u[v, i + 2, tile(t)], 2 * (t * ROWS + i) + 2, 1)
                packed[v] = jnp.where(group == i, moved, packed[v])
                packed[NV + v] = jnp.where(group == i + 1, moved, packed[NV + v])
        return tuple(packed)

    def keep_packed(slot, packed):
        for v in range(NV):
            pk[slot, 0, v] = packed[v]
            pk[slot, 1, v] = packed[NV + v]

    blank = (jnp.zeros((SUB, LANES), F32),) * (2 * NV)

    landed(u1.at[:, pl.ds(2, len(edge_rows))], in_sem.at[0])
    pl.semaphore_wait(barrier, len(greet))

    def circ_pair(ref, which, low, width):
        def part(start):
            return ref.at[pl.ds(start, width)]

        count = ROWS
        to_left = remote(part(low), part(low + count), circ_s.at[which, 0], circ_r.at[which, 0], left)
        to_right = remote(part(low + count - width), part(low - width), circ_s.at[which, 1], circ_r.at[which, 1], right)
        return [to_left, to_right]

    def axial_pair(slot):
        up = remote(pk.at[slot, 0], pkh.at[slot, 0], ax_s.at[slot, 0], ax_r.at[slot, 0], ax_up)
        down = remote(pk.at[slot, 1], pkh.at[slot, 1], ax_s.at[slot, 1], ax_r.at[slot, 1], ax_down)
        return [up, down]

    def chunk_pair(t):
        def part(start):
            return u1.at[:, pl.ds(start, 2), tile(t)]

        to_left = remote(part(2), part(ROWS + 2), uc_s.at[0, t], uc_r.at[0, t], left)
        to_right = remote(part(ROWS), part(0), uc_s.at[1, t], uc_r.at[1, t], right)
        return [to_left, to_right]

    pending = []

    def begin(copies):
        for copy in copies:
            copy.start()
        pending.extend(copies)
        return copies

    other = HALF * (1 - c)
    mine = HALF * c

    def chunk_send(step, carry):
        for copy in chunk_pair(around(step + mine, TILES)):
            copy.start()
        return carry

    lax.fori_loop(0, TILES, chunk_send, 0)
    ready_signal(0)
    load_cell(radius_ratio, rad, 1, 2)
    load_cell(inv_volume, vol, 0, 3)
    landed(u1.at[:, pl.ds(2, len(inner_rows))], in_sem.at[1])
    keep_packed(0, lax.fori_loop(0, TILES, functools.partial(pack, u1), blank))
    ax_halo = begin(axial_pair(0))
    for v in range(NV):
        for m in range(NV):
            tab[0, v, m] = jnp.broadcast_to(jac_c[v, m] / 12.0, (SUB, LANES))
            tab[1, v, m] = jnp.broadcast_to(0.5 * jac_o[v, 0, m], (SUB, LANES))
            tab[2, v, m] = jnp.broadcast_to(0.5 * jac_o[v, 1, m], (SUB, LANES))

    load_cell(time_step, dt, 2, 4)
    landed(rad.at[pl.ds(1, ROWS)], in_sem.at[2])
    landed(vol, in_sem.at[3])

    def splat(value):
        return jnp.broadcast_to(value, (SUB, LANES))

    def local_step(u, slot, t, carry):
        above = jnp.minimum(t * SUB + SUB, TILES * SUB - 1)
        below = jnp.maximum(t * SUB - 1, 0)
        for i in range(ROWS):
            total = [None] * NV
            for m in range(NV):

                def row(k):
                    return u[m, k + 2, tile(t)] if slot == 1 or 0 <= k < ROWS else None

                def minus(p, q):
                    if p is None:
                        return -q
                    return p if q is None else p - q

                centre = u[m, i + 2, tile(t)]
                circ = 8.0 * minus(row(i + 1), row(i - 1)) - minus(row(i + 2), row(i - 2))
                plus1 = pltpu.roll(centre, LANES - 1, 1)
                plus2 = pltpu.roll(centre, LANES - 2, 1)
                minus1 = pltpu.roll(centre, 1, 1)
                minus2 = pltpu.roll(centre, 2, 1)
                axial = plus1 - minus1
                fourth = (plus2 + minus2) - 4.0 * (plus1 + minus1) + 6.0 * centre
                over = jnp.where(
                    sub == SUB - 1, splat(u[m, i + 2, pl.ds(above, 1)]), pltpu.roll(centre, SUB - 1, 0)
                )
                under = jnp.where(sub == 0, splat(u[m, i + 2, pl.ds(below, 1)]), pltpu.roll(centre, 1, 0))
                normal = over - under
                for v in range(NV):
                    term = tab[0, v, m] * circ + tab[1, v, m] * axial + tab[2, v, m] * normal
                    if v == m:
                        term = term + DISSIPATION * fourth
                    total[v] = term if total[v] is None else total[v] + term
            for v in range(NV):
                yy[v, i, tile(t)] = total[v]
        return carry

    def mix(which, values):
        out_values = []
        for v in range(NV):
            total = tab[which, v, 0] * values[0]
            for m in range(1, NV):
                total = total + tab[which, v, m] * values[m]
            out_values.append(total)
        return out_values

    def edge_fluxes(slot):
        even = lane % 2 == 0
        low_edge = jnp.broadcast_to(a == 0, (SUB, LANES))
        high_edge = jnp.broadcast_to(a == na - 1, (SUB, LANES))
        low = [jnp.where(low_edge, 0.0, pkh[slot, 0, v]) - pk[slot, 0, v] for v in range(NV)]
        high = [
            pltpu.roll(jnp.where(high_edge, 0.0, pkh[slot, 1, v]) - pk[slot, 1, v], LANES - 2, 1) for v in range(NV)
        ]
        low_next = [pltpu.roll(value, LANES - 1, 1) for value in low]
        high_next = [pltpu.roll(value, 1, 1) for value in high]
        low_flux = mix(1, [jnp.where(even, -value, 0.0) for value in low_next])
        high_flux = mix(1, [jnp.where(even, 0.0, value) for value in high_next])
        for v in range(NV):
            low_total = low_flux[v] + DISSIPATION * jnp.where(even, low[v] - 4.0 * low_next[v], low[v])
            high_total = high_flux[v] + DISSIPATION * jnp.where(even, high[v], high[v] - 4.0 * high_next[v])
            for half in range(2):
                index = (lane // 4) * 2 + lane % 2 + half * (HALF * ROWS * 2)
                index = jnp.minimum(index, LANES - 1)
                picked_low = jnp.take_along_axis(low_total, index, axis=1)
                picked_high = jnp.take_along_axis(high_total, index, axis=1)
                edge[half, v] = jnp.where(lane % 4 < 2, picked_high, picked_low)

    def sweep_step(slot, t):
        if slot == 0:
            for copy in chunk_pair(t):
                copy.wait_recv()
            low2, low1, high1, high2 = ([u1[m, k, tile(t)] for m in range(NV)] for k in (0, 1, ROWS + 2, ROWS + 3))
            extra = {
                0: mix(0, [p - 8.0 * q for p, q in zip(low2, low1)]),
                1: mix(0, low1),
                ROWS - 2: mix(0, [-q for q in high1]),
                ROWS - 1: mix(0, [8.0 * q - p for p, q in zip(high2, high1)]),
            }
        near = (lane < 2) | (lane >= LANES - 2)
        half = lax.div(t, HALF)
        base = lax.rem(t, HALF) * ROWS
        ahead = [jnp.zeros((SUB, LANES), F32)] * NV
        start = [jnp.zeros((SUB, LANES), F32)] * NV
        product = jnp.ones((SUB, LANES), F32)
        for i in range(ROWS):
            weight = wgt[i, tile(t)]
            ratio = cc[i, tile(t)]
            for v in range(NV):
                flux = yy[v, i, tile(t)]
                if slot == 0 and i in extra:
                    flux = flux + extra[i][v]
                side = pltpu.roll(edge[half, v], LANES - 2 - 4 * (base + i), 1)
                scaled = weight * (flux + jnp.where(near, side, 0.0))
                if slot == 0 and i == 0:
                    qrow[0, v, tile(t)] = scaled
                if slot == 0 and i == ROWS - 1:
                    qrow[1, v, tile(t)] = scaled
                ahead[v] = (scaled + ahead[v]) * ratio
                yy[v, i, tile(t)] = ahead[v]
                start[v] = start[v] + product * ahead[v]
            product = cp[i, tile(t)]
        for v in range(NV):
            pb[slot, t, v, 0] = start[v]
            pb[slot, t, v, 1] = ahead[v]

    def factor_step(t, carry):
        ratio = jnp.zeros((SUB, LANES), F32)
        product = jnp.ones((SUB, LANES), F32)
        first = jnp.zeros((SUB, LANES), F32)
        for i in range(ROWS):
            inverse = inverse_smoothing(rad[i + 1, tile(t)])
            wgt[i, tile(t)] = -vol[i, tile(t)] * inverse
            ratio = 1.0 / (2.0 + inverse - ratio)
            cc[i, tile(t)] = ratio
            previous = product
            product = product * ratio
            cp[i, tile(t)] = product
            first = first + previous * product
        gg[t, 0] = first
        gg[t, 1] = product
        gg[t, 2] = ratio
        return carry

    lax.fori_loop(0, TILES, factor_step, 0)
    g_pair = begin([remote(gg.at[pl.ds(other, HALF)], gr, gp_s, gp_r, partner)])
    ready_wait(0)
    ready_signal(1)
    lax.fori_loop(0, SPLIT, functools.partial(local_step, u1, 0), 0)
    ready_wait(1)
    ready_signal(2)

    def by_core(own, theirs):
        return jnp.where(core0, own, theirs), jnp.where(core0, theirs, own)

    def join(a_first, a_cross, a_last, b_first, b_cross, b_last):
        d = 1.0 / (1.0 - a_last * b_first)
        return (
            d,
            a_first + a_cross * a_cross * d * b_first,
            a_cross * d * b_cross,
            b_last + b_cross * b_cross * d * a_last,
        )

    def inner_pair(alpha, beta, a_last, b_first, d):
        return d * (alpha + a_last * beta), d * (beta + b_first * alpha)

    g_pair[0].wait_recv()

    def merge_step(t, carry):
        pairs = [by_core(gg[mine + t, n], gr[t, n]) for n in range(3)]
        (a_first, b_first), (a_cross, b_cross), (a_last, b_last) = pairs
        d, first, cross, last = join(a_first, a_cross, a_last, b_first, b_cross, b_last)
        for n, value in enumerate((a_cross, a_last, b_first, b_cross, d)):
            gm[1, t, n] = value
        for n, value in enumerate((first, cross, last)):
            gm[0, t, n] = value
        return carry

    lax.fori_loop(0, HALF, merge_step, 0)

    def spread(src_of, dst, ssem, rsem, targets):
        for target in targets:

            @pl.when(target != me)
            def _(target=target):
                remote(src_of(target), dst.at[me], ssem, rsem, rank_device(target)).start()

    def group_recv(dst, rsem, count):
        part = dst.at[pl.ds(0, count)]
        remote(part, part, rsem, rsem, partner).wait_recv()

    def group_sent(src, ssem, count):
        part = src.at[pl.ds(0, count)]
        remote(part, part, ssem, ssem, partner).wait_send()

    def spread_end(src, ssem):
        @pl.when(me < UNITS)
        def _():
            group_sent(src, ssem, UNITS - 1)

        @pl.when(me >= UNITS)
        def _():
            group_sent(src, ssem, UNITS)

    def g_source(target):
        return gm.at[0, target // NV, pl.ds(0, 3)]

    ready_wait(2)
    spread(g_source, gt, ga_s, ga_r, range(UNITS))
    lax.fori_loop(SPLIT, TILES, functools.partial(local_step, u1, 0), 0)
    landed(dt.at[pl.ds(2, ROWS)], in_sem.at[4])

    def tree_factors():
        for r in range(ranks):
            for n in range(3):
                td[r, n] = gt[r, n]
        first, width, node = 0, ranks, ranks
        while width > 1:
            for k in range(0, width, 2):
                left_node, right_node = first + k, first + k + 1
                d, g0, g1, g2 = join(*(td[left_node, n] for n in range(3)), *(td[right_node, n] for n in range(3)))
                for n, value in enumerate((g0, g1, g2, d)):
                    td[node, n] = value
                node += 1
            first, width = first + width, width // 2
        top = 2 * ranks - 2
        inner = 1.0 - td[top, 1]
        td[top + 1, 0] = 1.0 / (inner * inner - td[top, 0] * td[top, 2])

    def tree_solve(slot):
        levels = []
        first, width, node = 0, ranks, ranks
        for r in range(ranks):
            for n in range(2):
                tp[r, n] = rb[slot, r, n]
        while width > 1:
            for k in range(0, width, 2):
                ln, rn = first + k, first + k + 1
                a0, b0 = inner_pair(tp[ln, 1], tp[rn, 0], td[ln, 2], td[rn, 0], td[node, 3])
                tp[node, 0] = tp[ln, 0] + td[ln, 1] * b0
                tp[node, 1] = tp[rn, 1] + td[rn, 1] * a0
                levels.append((node, ln, rn))
                node += 1
            first, width = first + width, width // 2
        top = 2 * ranks - 2
        inner = 1.0 - td[top, 1]
        det = td[top + 1, 0]
        tx[top, 0] = (inner * tp[top, 1] + td[top, 2] * tp[top, 0]) * det
        tx[top, 1] = (inner * tp[top, 0] + td[top, 0] * tp[top, 1]) * det
        for node, ln, rn in levels[::-1]:
            xl, xh = tx[node, 0], tx[node, 1]
            alpha = tp[ln, 1] + td[ln, 1] * xl
            beta = tp[rn, 0] + td[rn, 1] * xh
            mid_a, mid_b = inner_pair(alpha, beta, td[ln, 2], td[rn, 0], td[node, 3])
            tx[ln, 0] = xl
            tx[ln, 1] = mid_b
            tx[rn, 0] = mid_a
            tx[rn, 1] = xh
        for r in range(ranks):
            for n in range(2):
                xb[slot, r, n] = tx[r, n]

    def pair_copy(slot, step):
        return remote(
            pb.at[slot, other + step], pr.at[slot, step], pp_s.at[slot, step], pp_r.at[slot, step], partner
        )

    def back_copy(slot, step):
        return remote(
            res.at[slot, step], xx.at[slot, mine + step], xp_s.at[slot, step], xp_r.at[slot, step], partner
        )

    def arrival(slot, step):
        return remote(
            res.at[slot, step], xx.at[slot, other + step], xp_s.at[slot, step], xp_r.at[slot, step], partner
        )

    def section_sent(slot):
        spread_end(mb.at[slot], pa_s.at[slot])

        @pl.when(me < UNITS)
        def _():
            group_sent(xb.at[slot], xa_s.at[slot], ranks - 1)

        for step in range(HALF):
            pair_copy(slot, step).wait_send()
            back_copy(slot, step).wait_send()

    def first_sent():
        for copy in pending:
            copy.wait_send()
        pending.clear()
        spread_end(gt, ga_s)

        def sent(t, carry):
            for copy in chunk_pair(t):
                copy.wait_send()
            return carry

        lax.fori_loop(0, TILES, sent, 0)
        section_sent(0)

    def section(slot):
        edge_fluxes(slot)

        def theirs(step, carry):
            sweep_step(slot, other + step)
            pair_copy(slot, step).start()
            return carry

        lax.fori_loop(0, HALF, theirs, 0)

        def ours(step, carry):
            sweep_step(slot, mine + step)
            pair_copy(slot, step).wait_recv()
            a_cross, a_last, b_first, b_cross, d = (gm[1, step, n] for n in range(5))
            for v in range(NV):
                a_head, b_head = by_core(pb[slot, mine + step, v, 0], pr[slot, step, v, 0])
                a_tail, b_tail = by_core(pb[slot, mine + step, v, 1], pr[slot, step, v, 1])
                a0, b0 = inner_pair(a_tail, b_head, a_last, b_first, d)
                mb[slot, step * NV + v, 0] = a_head + a_cross * b0
                mb[slot, step * NV + v, 1] = b_tail + b_cross * a0
            spread(
                lambda target: mb.at[slot, target],
                rb.at[slot],
                pa_s.at[slot],
                pa_r.at[slot],
                [step * NV + v for v in range(NV)],
            )
            return carry

        lax.fori_loop(0, HALF, ours, 0)

        q_halo = []
        if slot == 0:
            q_halo = begin(
                circ_pair(rad, 0, 1, 1)
                + circ_pair(dt, 1, 2, 2)
                + [
                    remote(qrow.at[0], qhalo.at[1], q_s.at[0], q_r.at[0], left),
                    remote(qrow.at[1], qhalo.at[0], q_s.at[1], q_r.at[1], right),
                ]
            )

        if slot == 1:
            first_sent()

        @pl.when(me < UNITS)
        def _():
            if slot == 0:
                gt[me] = gm[0, lax.div(me, NV), pl.ds(0, 3)]
                group_recv(gt, ga_r, ranks - 1)
                tree_factors()
            rb[slot, me] = mb[slot, me]
            group_recv(rb.at[slot], pa_r.at[slot], ranks - 1)
            tree_solve(slot)
            xr[slot, me] = xb[slot, me]
            for n in range(len(offsets)):
                plane, column = peer(n)
                remote(
                    xb.at[slot, plane * 2 + column],
                    xr.at[slot, me],
                    xa_s.at[slot],
                    xa_r.at[slot, lax.div(me, NV)],
                    plane_device(plane, column),
                ).start()

        def unmerge(step, carry):
            @pl.when(lax.div(me, NV) == step)
            def _():
                group_recv(xr.at[slot], xa_r.at[slot, step], NV - 1)

            @pl.when(lax.div(me, NV) != step)
            def _():
                group_recv(xr.at[slot], xa_r.at[slot, step], NV)

            a_cross, a_last, b_first, b_cross, d = (gm[1, step, n] for n in range(5))
            for v in range(NV):
                xl, xh = xr[slot, step * NV + v, 0], xr[slot, step * NV + v, 1]
                _, b_head = by_core(pb[slot, mine + step, v, 0], pr[slot, step, v, 0])
                a_tail, _ = by_core(pb[slot, mine + step, v, 1], pr[slot, step, v, 1])
                mid_a, mid_b = inner_pair(a_tail + a_cross * xl, b_head + b_cross * xh, a_last, b_first, d)
                xx[slot, mine + step, v, 0] = jnp.where(core0, xl, mid_a)
                xx[slot, mine + step, v, 1] = jnp.where(core0, mid_b, xh)
                res[slot, step, v, 0] = jnp.where(core0, mid_a, xl)
                res[slot, step, v, 1] = jnp.where(core0, xh, mid_b)
            back_copy(slot, step).start()
            return carry

        lax.fori_loop(0, HALF, unmerge, 0)
        return q_halo

    def sweep(slot, t, v):
        low, high = xx[slot, t, v, 0], xx[slot, t, v, 1]
        values = [None] * ROWS
        later = high
        for i in range(ROWS - 1, -1, -1):
            later = yy[v, i, tile(t)] + cp[i, tile(t)] * low + cc[i, tile(t)] * later
            values[i] = later
        return low, high, values

    for copy in ax_halo:
        copy.wait_recv()
    q_halo = section(0)
    for copy in q_halo:
        copy.wait_recv()

    def update_one(t, carry):
        diag_low = 2.0 + inverse_smoothing(rad[0, tile(t)])
        diag_high = 2.0 + inverse_smoothing(rad[ROWS + 1, tile(t)])
        for v in range(NV):
            low, high, values = sweep(0, t, v)
            low2 = diag_low * low - values[0] - qhalo[0, v, tile(t)]
            high2 = diag_high * high - values[ROWS - 1] - qhalo[1, v, tile(t)]
            for i, value in enumerate([low2, low] + values + [high, high2]):
                u2[v, i, tile(t)] = u1[v, i, tile(t)] + SECTION_ONE * dt[i, tile(t)] * value
        return pack(u2, t, carry)

    def update_one_late(step, carry):
        arrival(0, step).wait_recv()
        return update_one(other + step, carry)

    packed = lax.fori_loop(0, HALF, lambda step, carry: update_one(mine + step, carry), blank)
    packed = lax.fori_loop(0, HALF, update_one_late, packed)
    keep_packed(1, packed)
    ax_halo = begin(axial_pair(1))
    lax.fori_loop(0, TILES, functools.partial(local_step, u2, 1), 0)
    for copy in ax_halo:
        copy.wait_recv()
    section(1)

    def update_two(t, carry):
        for v in range(NV):
            _, _, values = sweep(1, t, v)
            for i, value in enumerate(values):
                start = pl.multiple_of((v * TILES + t) * (SUB * ROWS), SUB) + i
                out[pl.ds(start, SUB, stride=ROWS), :] = u1[v, i + 2, tile(t)] + dt[i + 2, tile(t)] * value
        return carry

    def update_two_late(step, carry):
        arrival(1, step).wait_recv()
        return update_two(other + step, carry)

    lax.fori_loop(0, HALF, lambda step, carry: update_two(mine + step, carry), 0)
    lax.fori_loop(0, HALF, update_two_late, 0)
    section_sent(1)


def solution(mesh):
    count = mesh.shape["blk"]
    nz, na = count // 4, mesh.shape["axial"]
    split = Mesh(mesh.devices.reshape(nz, 2, 2, na), (*BLK, "axial"))
    ranks = nz * 2

    def on_device(fields, inv_volume, radius_ratio, time_step, jac_circ, jac_other):
        layers = fields.shape[1]
        vmem = lambda *shape: pltpu.VMEM(shape, F32)
        dma = lambda *shape: pltpu.SemaphoreType.DMA(shape)
        plane = (layers, LANES)
        cell = (SUB, LANES)
        scratch = [
            vmem(NV, ROWS + 4, *plane),
            vmem(NV, ROWS + 4, *plane),
            vmem(ROWS, *plane),
            vmem(ROWS + 2, *plane),
            vmem(ROWS + 4, *plane),
            vmem(ROWS, *plane),
            vmem(ROWS, *plane),
            vmem(ROWS, *plane),
            vmem(NV, ROWS, *plane),
            vmem(2, NV, *plane),
            vmem(2, NV, *plane),
            vmem(2, 2, NV, *cell),
            vmem(2, 2, NV, *cell),
            vmem(2, TILES, NV, 2, *cell),
            vmem(2, HALF, NV, 2, *cell),
            vmem(2, UNITS, 2, *cell),
            vmem(2, ranks, 2, *cell),
            vmem(2, ranks, 2, *cell),
            vmem(2, UNITS, 2, *cell),
            vmem(2, TILES, NV, 2, *cell),
            vmem(TILES, 3, *cell),
            vmem(HALF, 3, *cell),
            vmem(2, HALF, 5, *cell),
            vmem(ranks, 3, *cell),
            vmem(2 * ranks, 4, *cell),
            vmem(2 * ranks, 2, *cell),
            vmem(2 * ranks, 2, *cell),
            vmem(2, HALF, NV, 2, *cell),
            vmem(3, NV, NV, *cell),
            vmem(2, NV, *cell),
            dma(5),
            dma(2, TILES),
            dma(2, TILES),
            dma(2, 2),
            dma(2, 2),
            dma(2, 2),
            dma(2, 2),
            dma(2),
            dma(2),
            pltpu.SemaphoreType.DMA,
            pltpu.SemaphoreType.DMA,
            pltpu.SemaphoreType.DMA,
            pltpu.SemaphoreType.DMA,
            dma(2, HALF),
            dma(2, HALF),
            dma(2),
            dma(2),
            dma(2),
            dma(2, HALF),
            dma(2, HALF),
            dma(2, HALF),
            pltpu.SemaphoreType.REGULAR((3,)),
        ]
        anywhere = pl.BlockSpec(memory_space=pl.ANY)
        scalars = pl.BlockSpec(memory_space=pltpu.SMEM)
        rows = fields.shape[0] * layers * fields.shape[2]
        operands = (fields, inv_volume, radius_ratio, time_step, jac_circ, jnp.transpose(jac_other, (1, 0, 2)))
        result = pl.pallas_call(
            functools.partial(kernel, nz, na),
            out_shape=jax.ShapeDtypeStruct((rows, LANES), F32),
            in_specs=[anywhere] * 4 + [scalars] * 2,
            out_specs=pl.BlockSpec(memory_space=pltpu.VMEM),
            scratch_shapes=scratch,
            compiler_params=pltpu.CompilerParams(
                collective_id=0, has_side_effects=True, vmem_limit_bytes=24 * 1024 * 1024
            ),
        )(*(pltpu.with_memory_space_constraint(x, pltpu.HBM) for x in operands))
        return result.reshape(fields.shape)

    return jax.shard_map(
        on_device,
        mesh=split,
        in_specs=(
            P(None, None, BLK, "axial"),
            P(None, BLK, "axial"),
            P(None, BLK, "axial"),
            P(None, BLK, "axial"),
            P(),
            P(),
        ),
        out_specs=P(None, None, BLK, "axial"),
        check_vma=False,
    )
```

```python
import functools

import jax
import jax.numpy as jnp
from jax import lax
from jax.experimental import pallas as pl
from jax.experimental.pallas import tpu as pltpu
from jax.sharding import Mesh
from jax.sharding import PartitionSpec as P

BLK = ("blk_0", "blk_1", "blk_2")
DISSIPATION = 0.03125
SECTION_ONE = 0.6
COURANT_RATIO = 2.0
SCALING_POWER = 2.0 / 3.0

NV = 5
TILES = 6
HALF = 3
ROWS = 8
SUB = 8
SPLIT = 2
LANES = 128
UNITS = HALF * NV
F32 = jnp.float32


def kernel(
    nz,
    na,
    fields,
    inv_volume,
    radius_ratio,
    time_step,
    jac_c,
    jac_o,
    out,
    u1,
    u2,
    vol,
    rad,
    dt,
    wgt,
    cc,
    cp,
    yy,
    qrow,
    qhalo,
    pk,
    pkh,
    pb,
    pr,
    mb,
    rb,
    xb,
    xr,
    xx,
    gg,
    gr,
    gm,
    gt,
    td,
    tp,
    tx,
    res,
    tab,
    edge,
    in_sem,
    uc_s,
    uc_r,
    circ_s,
    circ_r,
    ax_s,
    ax_r,
    q_s,
    q_r,
    gp_s,
    gp_r,
    ga_s,
    ga_r,
    pp_s,
    pp_r,
    pa_s,
    pa_r,
    xa_s,
    xa_r,
    xp_s,
    xp_r,
    ready,
):
    ranks = nz * 2
    z = lax.axis_index("blk_0")
    y = lax.axis_index("blk_1")
    c = lax.axis_index("blk_2")
    a = lax.axis_index("axial")
    me = z * 2 + y

    def blk_device(b):
        return {"blk_0": lax.div(b, 4), "blk_1": lax.rem(lax.div(b, 2), 2), "blk_2": lax.rem(b, 2), "axial": a}

    def ax_device(index):
        return {"blk_0": z, "blk_1": y, "blk_2": c, "axial": index}

    def rank_device(rank):
        if isinstance(rank, int):
            return {"blk_0": rank // 2, "blk_1": rank % 2, "blk_2": c, "axial": a}
        return {"blk_0": lax.div(rank, 2), "blk_1": lax.rem(rank, 2), "blk_2": c, "axial": a}

    def plane_device(plane, column):
        return {"blk_0": plane, "blk_1": column, "blk_2": c, "axial": a}

    def around(value, count):
        return lax.rem(value, count)

    b = me * 2 + c
    size = ranks * 2
    right = blk_device(around(b + 1, size))
    left = blk_device(around(b + size - 1, size))
    ax_up = ax_device(around(a + 1, na))
    ax_down = ax_device(around(a + na - 1, na))
    partner = {"blk_0": z, "blk_1": y, "blk_2": 1 - c, "axial": a}
    hops = [dz for k in range(nz // 2, 0, -1) for dz in dict.fromkeys((k, nz - k))] + [0]
    offsets = [(dz, dy) for dz in hops for dy in (1, 0) if (dz, dy) != (0, 0)]

    def peer(n):
        dz, dy = offsets[n]
        return around(z + dz, nz), (1 - y if dy else y)

    def remote(src, dst, ssem, rsem, device):
        return pltpu.make_async_remote_copy(
            src_ref=src,
            dst_ref=dst,
            send_sem=ssem,
            recv_sem=rsem,
            device_id=device,
            device_id_type=pl.DeviceIdType.MESH,
        )

    def load_u(i, group):
        pltpu.make_async_copy(fields.at[:, :, i, :], u1.at[:, i + 2], in_sem.at[group]).start()

    def load_cell(source_ref, target_ref, shift, group):
        for i in range(ROWS):
            pltpu.make_async_copy(source_ref.at[:, i, :], target_ref.at[i + shift], in_sem.at[group]).start()

    def landed(part, semaphore):
        pltpu.make_async_copy(part, part, semaphore).wait()

    def beside(dz, dy):
        return plane_device(around(z + nz + dz, nz), 1 - y if dy else y)

    def signal(semaphore, device):
        pl.semaphore_signal(semaphore, inc=1, device_id=device, device_id_type=pl.DeviceIdType.MESH)

    barrier = pltpu.get_barrier_semaphore()
    greet = [right, left, beside(1, 1), beside(-1, 1), beside(1, 0), beside(-1, 0), beside(0, 1), partner]
    edge_rows, inner_rows = (0, 1, ROWS - 2, ROWS - 1), range(2, ROWS - 2)
    for i in edge_rows:
        load_u(i, 0)
    pl.when(a < na - 1)(lambda: signal(barrier, ax_up))
    pl.when(a > 0)(lambda: signal(barrier, ax_down))
    for device in greet:
        signal(barrier, device)
    for i in inner_rows:
        load_u(i, 1)

    def ready_signal(n):
        for dz in (1, -1):
            signal(ready.at[n], beside(dz, 0))

    def ready_wait(n):
        pl.semaphore_wait(ready.at[n], 2)

    lane = lax.broadcasted_iota(jnp.int32, (SUB, LANES), 1)
    sub = lax.broadcasted_iota(jnp.int32, (SUB, LANES), 0)
    core0 = jnp.broadcast_to(c == 0, (SUB, LANES))

    def tile(t):
        return pl.ds(pl.multiple_of(t * SUB, SUB), SUB)

    def inverse_smoothing(ratio):
        scaled = COURANT_RATIO * (1.0 + jnp.exp(SCALING_POWER * jnp.log(ratio)))
        return 1.0 / (0.25 * (scaled * scaled - 1.0))

    def pack(u, t, carry):
        packed = list(carry)
        group = lane // 2 - t * ROWS
        for v in range(NV):
            for i in range(ROWS):
                moved = pltpu.roll(u[v, i + 2, tile(t)], 2 * (t * ROWS + i) + 2, 1)
                packed[v] = jnp.where(group == i, moved, packed[v])
                packed[NV + v] = jnp.where(group == i + 1, moved, packed[NV + v])
        return tuple(packed)

    def keep_packed(slot, packed):
        for v in range(NV):
            pk[slot, 0, v] = packed[v]
            pk[slot, 1, v] = packed[NV + v]

    blank = (jnp.zeros((SUB, LANES), F32),) * (2 * NV)

    landed(u1.at[:, pl.ds(2, len(edge_rows))], in_sem.at[0])
    pl.semaphore_wait(barrier, len(greet) + jnp.minimum(a, 1) + jnp.minimum(na - 1 - a, 1))

    def circ_pair(ref, which, low, width):
        def part(start):
            return ref.at[pl.ds(start, width)]

        count = ROWS
        to_left = remote(part(low), part(low + count), circ_s.at[which, 0], circ_r.at[which, 0], left)
        to_right = remote(part(low + count - width), part(low - width), circ_s.at[which, 1], circ_r.at[which, 1], right)
        return [to_left, to_right]

    def axial_pair(slot):
        up = remote(pk.at[slot, 0], pkh.at[slot, 0], ax_s.at[slot, 0], ax_r.at[slot, 0], ax_up)
        down = remote(pk.at[slot, 1], pkh.at[slot, 1], ax_s.at[slot, 1], ax_r.at[slot, 1], ax_down)
        return [up, down]

    def chunk_pair(t):
        def part(start):
            return u1.at[:, pl.ds(start, 2), tile(t)]

        to_left = remote(part(2), part(ROWS + 2), uc_s.at[0, t], uc_r.at[0, t], left)
        to_right = remote(part(ROWS), part(0), uc_s.at[1, t], uc_r.at[1, t], right)
        return [to_left, to_right]

    pending = []
    axial_pending = []

    class Axial:
        def __init__(self, pair):
            self.up, self.down = pair

        def start(self):
            pl.when(a < na - 1)(self.up.start)
            pl.when(a > 0)(self.down.start)
            axial_pending.append(self)
            return self

        def wait_recv(self):
            pl.when(a > 0)(self.up.wait_recv)
            pl.when(a < na - 1)(self.down.wait_recv)

        def wait_send(self):
            pl.when(a < na - 1)(self.up.wait_send)
            pl.when(a > 0)(self.down.wait_send)


    def begin(copies):
        for copy in copies:
            copy.start()
        pending.extend(copies)
        return copies

    other = HALF * (1 - c)
    mine = HALF * c

    def chunk_send(step, carry):
        for copy in chunk_pair(around(step + mine, TILES)):
            copy.start()
        return carry

    lax.fori_loop(0, TILES, chunk_send, 0)
    ready_signal(0)
    load_cell(radius_ratio, rad, 1, 2)
    load_cell(inv_volume, vol, 0, 3)
    landed(u1.at[:, pl.ds(2, len(inner_rows))], in_sem.at[1])
    keep_packed(0, lax.fori_loop(0, TILES, functools.partial(pack, u1), blank))
    ax_halo = Axial(axial_pair(0)).start()

    @pl.when(a == 0)
    def _():
        for slot in range(2):
            pkh[slot, 0] = jnp.zeros((NV, SUB, LANES), F32)

    @pl.when(a == na - 1)
    def _():
        for slot in range(2):
            pkh[slot, 1] = jnp.zeros((NV, SUB, LANES), F32)

    for v in range(NV):
        for m in range(NV):
            tab[0, v, m] = jnp.broadcast_to(jac_c[v, m] / 12.0, (SUB, LANES))
            tab[1, v, m] = jnp.broadcast_to(0.5 * jac_o[v, 0, m], (SUB, LANES))
            tab[2, v, m] = jnp.broadcast_to(0.5 * jac_o[v, 1, m], (SUB, LANES))

    load_cell(time_step, dt, 2, 4)
    landed(rad.at[pl.ds(1, ROWS)], in_sem.at[2])
    landed(vol, in_sem.at[3])

    def splat(value):
        return jnp.broadcast_to(value, (SUB, LANES))

    def local_step(u, slot, t, carry):
        above = jnp.minimum(t * SUB + SUB, TILES * SUB - 1)
        below = jnp.maximum(t * SUB - 1, 0)
        for i in range(ROWS):
            total = [None] * NV
            for m in range(NV):

                def row(k):
                    return u[m, k + 2, tile(t)] if slot == 1 or 0 <= k < ROWS else None

                def minus(p, q):
                    if p is None:
                        return -q
                    return p if q is None else p - q

                centre = u[m, i + 2, tile(t)]
                circ = 8.0 * minus(row(i + 1), row(i - 1)) - minus(row(i + 2), row(i - 2))
                plus1 = pltpu.roll(centre, LANES - 1, 1)
                plus2 = pltpu.roll(centre, LANES - 2, 1)
                minus1 = pltpu.roll(centre, 1, 1)
                minus2 = pltpu.roll(centre, 2, 1)
                axial = plus1 - minus1
                fourth = (plus2 + minus2) - 4.0 * (plus1 + minus1) + 6.0 * centre
                over = jnp.where(
                    sub == SUB - 1, splat(u[m, i + 2, pl.ds(above, 1)]), pltpu.roll(centre, SUB - 1, 0)
                )
                under = jnp.where(sub == 0, splat(u[m, i + 2, pl.ds(below, 1)]), pltpu.roll(centre, 1, 0))
                normal = over - under
                for v in range(NV):
                    term = tab[0, v, m] * circ + tab[1, v, m] * axial + tab[2, v, m] * normal
                    if v == m:
                        term = term + DISSIPATION * fourth
                    total[v] = term if total[v] is None else total[v] + term
            for v in range(NV):
                yy[v, i, tile(t)] = total[v]
        return carry

    def mix(which, values):
        out_values = []
        for v in range(NV):
            total = tab[which, v, 0] * values[0]
            for m in range(1, NV):
                total = total + tab[which, v, m] * values[m]
            out_values.append(total)
        return out_values

    def edge_fluxes(slot):
        even = lane % 2 == 0
        low_edge = jnp.broadcast_to(a == 0, (SUB, LANES))
        high_edge = jnp.broadcast_to(a == na - 1, (SUB, LANES))
        low = [jnp.where(low_edge, 0.0, pkh[slot, 0, v]) - pk[slot, 0, v] for v in range(NV)]
        high = [
            pltpu.roll(jnp.where(high_edge, 0.0, pkh[slot, 1, v]) - pk[slot, 1, v], LANES - 2, 1) for v in range(NV)
        ]
        low_next = [pltpu.roll(value, LANES - 1, 1) for value in low]
        high_next = [pltpu.roll(value, 1, 1) for value in high]
        low_flux = mix(1, [jnp.where(even, -value, 0.0) for value in low_next])
        high_flux = mix(1, [jnp.where(even, 0.0, value) for value in high_next])
        for v in range(NV):
            low_total = low_flux[v] + DISSIPATION * jnp.where(even, low[v] - 4.0 * low_next[v], low[v])
            high_total = high_flux[v] + DISSIPATION * jnp.where(even, high[v], high[v] - 4.0 * high_next[v])
            for half in range(2):
                index = (lane // 4) * 2 + lane % 2 + half * (HALF * ROWS * 2)
                index = jnp.minimum(index, LANES - 1)
                picked_low = jnp.take_along_axis(low_total, index, axis=1)
                picked_high = jnp.take_along_axis(high_total, index, axis=1)
                edge[half, v] = jnp.where(lane % 4 < 2, picked_high, picked_low)

    def sweep_step(slot, t):
        if slot == 0:
            for copy in chunk_pair(t):
                copy.wait_recv()
            low2, low1, high1, high2 = ([u1[m, k, tile(t)] for m in range(NV)] for k in (0, 1, ROWS + 2, ROWS + 3))
            extra = {
                0: mix(0, [p - 8.0 * q for p, q in zip(low2, low1)]),
                1: mix(0, low1),
                ROWS - 2: mix(0, [-q for q in high1]),
                ROWS - 1: mix(0, [8.0 * q - p for p, q in zip(high2, high1)]),
            }
        near = (lane < 2) | (lane >= LANES - 2)
        half = lax.div(t, HALF)
        base = lax.rem(t, HALF) * ROWS
        ahead = [jnp.zeros((SUB, LANES), F32)] * NV
        start = [jnp.zeros((SUB, LANES), F32)] * NV
        product = jnp.ones((SUB, LANES), F32)
        for i in range(ROWS):
            weight = wgt[i, tile(t)]
            ratio = cc[i, tile(t)]
            for v in range(NV):
                flux = yy[v, i, tile(t)]
                if slot == 0 and i in extra:
                    flux = flux + extra[i][v]
                side = pltpu.roll(edge[half, v], LANES - 2 - 4 * (base + i), 1)
                scaled = weight * (flux + jnp.where(near, side, 0.0))
                if slot == 0 and i == 0:
                    qrow[0, v, tile(t)] = scaled
                if slot == 0 and i == ROWS - 1:
                    qrow[1, v, tile(t)] = scaled
                ahead[v] = (scaled + ahead[v]) * ratio
                yy[v, i, tile(t)] = ahead[v]
                start[v] = start[v] + product * ahead[v]
            product = cp[i, tile(t)]
        for v in range(NV):
            pb[slot, t, v, 0] = start[v]
            pb[slot, t, v, 1] = ahead[v]

    def factor_step(t, carry):
        ratio = jnp.zeros((SUB, LANES), F32)
        product = jnp.ones((SUB, LANES), F32)
        first = jnp.zeros((SUB, LANES), F32)
        for i in range(ROWS):
            inverse = inverse_smoothing(rad[i + 1, tile(t)])
            wgt[i, tile(t)] = -vol[i, tile(t)] * inverse
            ratio = 1.0 / (2.0 + inverse - ratio)
            cc[i, tile(t)] = ratio
            previous = product
            product = product * ratio
            cp[i, tile(t)] = product
            first = first + previous * product
        gg[t, 0] = first
        gg[t, 1] = product
        gg[t, 2] = ratio
        return carry

    lax.fori_loop(0, TILES, factor_step, 0)
    g_pair = begin([remote(gg.at[pl.ds(other, HALF)], gr, gp_s, gp_r, partner)])
    ready_wait(0)
    ready_signal(1)
    lax.fori_loop(0, SPLIT, functools.partial(local_step, u1, 0), 0)
    ready_wait(1)
    ready_signal(2)

    def by_core(own, theirs):
        return jnp.where(core0, own, theirs), jnp.where(core0, theirs, own)

    def join(a_first, a_cross, a_last, b_first, b_cross, b_last):
        d = 1.0 / (1.0 - a_last * b_first)
        return (
            d,
            a_first + a_cross * a_cross * d * b_first,
            a_cross * d * b_cross,
            b_last + b_cross * b_cross * d * a_last,
        )

    def inner_pair(alpha, beta, a_last, b_first, d):
        return d * (alpha + a_last * beta), d * (beta + b_first * alpha)

    g_pair[0].wait_recv()

    def merge_step(t, carry):
        pairs = [by_core(gg[mine + t, n], gr[t, n]) for n in range(3)]
        (a_first, b_first), (a_cross, b_cross), (a_last, b_last) = pairs
        d, first, cross, last = join(a_first, a_cross, a_last, b_first, b_cross, b_last)
        for n, value in enumerate((a_cross, a_last, b_first, b_cross, d)):
            gm[1, t, n] = value
        for n, value in enumerate((first, cross, last)):
            gm[0, t, n] = value
        return carry

    lax.fori_loop(0, HALF, merge_step, 0)

    def spread(src_of, dst, ssem, rsem, targets):
        for target in targets:

            @pl.when(target != me)
            def _(target=target):
                remote(src_of(target), dst.at[me], ssem, rsem, rank_device(target)).start()

    def group_recv(dst, rsem, count):
        part = dst.at[pl.ds(0, count)]
        remote(part, part, rsem, rsem, partner).wait_recv()

    def group_sent(src, ssem, count):
        part = src.at[pl.ds(0, count)]
        remote(part, part, ssem, ssem, partner).wait_send()

    def spread_end(src, ssem):
        @pl.when(me < UNITS)
        def _():
            group_sent(src, ssem, UNITS - 1)

        @pl.when(me >= UNITS)
        def _():
            group_sent(src, ssem, UNITS)

    def g_source(target):
        return gm.at[0, target // NV, pl.ds(0, 3)]

    ready_wait(2)
    spread(g_source, gt, ga_s, ga_r, range(UNITS))
    lax.fori_loop(SPLIT, TILES, functools.partial(local_step, u1, 0), 0)
    landed(dt.at[pl.ds(2, ROWS)], in_sem.at[4])

    def tree_factors():
        for r in range(ranks):
            for n in range(3):
                td[r, n] = gt[r, n]
        first, width, node = 0, ranks, ranks
        while width > 1:
            for k in range(0, width, 2):
                left_node, right_node = first + k, first + k + 1
                d, g0, g1, g2 = join(*(td[left_node, n] for n in range(3)), *(td[right_node, n] for n in range(3)))
                for n, value in enumerate((g0, g1, g2, d)):
                    td[node, n] = value
                node += 1
            first, width = first + width, width // 2
        top = 2 * ranks - 2
        inner = 1.0 - td[top, 1]
        td[top + 1, 0] = 1.0 / (inner * inner - td[top, 0] * td[top, 2])

    def tree_solve(slot):
        levels = []
        first, width, node = 0, ranks, ranks
        for r in range(ranks):
            for n in range(2):
                tp[r, n] = rb[slot, r, n]
        while width > 1:
            for k in range(0, width, 2):
                ln, rn = first + k, first + k + 1
                a0, b0 = inner_pair(tp[ln, 1], tp[rn, 0], td[ln, 2], td[rn, 0], td[node, 3])
                tp[node, 0] = tp[ln, 0] + td[ln, 1] * b0
                tp[node, 1] = tp[rn, 1] + td[rn, 1] * a0
                levels.append((node, ln, rn))
                node += 1
            first, width = first + width, width // 2
        top = 2 * ranks - 2
        inner = 1.0 - td[top, 1]
        det = td[top + 1, 0]
        tx[top, 0] = (inner * tp[top, 1] + td[top, 2] * tp[top, 0]) * det
        tx[top, 1] = (inner * tp[top, 0] + td[top, 0] * tp[top, 1]) * det
        for node, ln, rn in levels[::-1]:
            xl, xh = tx[node, 0], tx[node, 1]
            alpha = tp[ln, 1] + td[ln, 1] * xl
            beta = tp[rn, 0] + td[rn, 1] * xh
            mid_a, mid_b = inner_pair(alpha, beta, td[ln, 2], td[rn, 0], td[node, 3])
            tx[ln, 0] = xl
            tx[ln, 1] = mid_b
            tx[rn, 0] = mid_a
            tx[rn, 1] = xh
        for r in range(ranks):
            for n in range(2):
                xb[slot, r, n] = tx[r, n]

    def pair_copy(slot, step):
        return remote(
            pb.at[slot, other + step], pr.at[slot, step], pp_s.at[slot, step], pp_r.at[slot, step], partner
        )

    def back_copy(slot, step):
        return remote(
            res.at[slot, step], xx.at[slot, mine + step], xp_s.at[slot, step], xp_r.at[slot, step], partner
        )

    def arrival(slot, step):
        return remote(
            res.at[slot, step], xx.at[slot, other + step], xp_s.at[slot, step], xp_r.at[slot, step], partner
        )

    def section_sent(slot):
        spread_end(mb.at[slot], pa_s.at[slot])

        @pl.when(me < UNITS)
        def _():
            group_sent(xb.at[slot], xa_s.at[slot], ranks - 1)

        for step in range(HALF):
            pair_copy(slot, step).wait_send()
            back_copy(slot, step).wait_send()

    def first_sent():
        for copy in pending:
            copy.wait_send()
        pending.clear()
        for copy in axial_pending:
            copy.wait_send()
        axial_pending.clear()
        spread_end(gt, ga_s)

        def sent(t, carry):
            for copy in chunk_pair(t):
                copy.wait_send()
            return carry

        lax.fori_loop(0, TILES, sent, 0)
        section_sent(0)

    def section(slot):
        edge_fluxes(slot)

        def theirs(step, carry):
            sweep_step(slot, other + step)
            pair_copy(slot, step).start()
            return carry

        lax.fori_loop(0, HALF, theirs, 0)

        def ours(step, carry):
            sweep_step(slot, mine + step)
            pair_copy(slot, step).wait_recv()
            a_cross, a_last, b_first, b_cross, d = (gm[1, step, n] for n in range(5))
            for v in range(NV):
                a_head, b_head = by_core(pb[slot, mine + step, v, 0], pr[slot, step, v, 0])
                a_tail, b_tail = by_core(pb[slot, mine + step, v, 1], pr[slot, step, v, 1])
                a0, b0 = inner_pair(a_tail, b_head, a_last, b_first, d)
                mb[slot, step * NV + v, 0] = a_head + a_cross * b0
                mb[slot, step * NV + v, 1] = b_tail + b_cross * a0
            spread(
                lambda target: mb.at[slot, target],
                rb.at[slot],
                pa_s.at[slot],
                pa_r.at[slot],
                [step * NV + v for v in range(NV)],
            )
            return carry

        lax.fori_loop(0, HALF, ours, 0)

        q_halo = []
        if slot == 0:
            q_halo = begin(
                circ_pair(rad, 0, 1, 1)
                + circ_pair(dt, 1, 2, 2)
                + [
                    remote(qrow.at[0], qhalo.at[1], q_s.at[0], q_r.at[0], left),
                    remote(qrow.at[1], qhalo.at[0], q_s.at[1], q_r.at[1], right),
                ]
            )

        if slot == 1:
            first_sent()

        @pl.when(me < UNITS)
        def _():
            if slot == 0:
                gt[me] = gm[0, lax.div(me, NV), pl.ds(0, 3)]
                group_recv(gt, ga_r, ranks - 1)
                tree_factors()
            rb[slot, me] = mb[slot, me]
            group_recv(rb.at[slot], pa_r.at[slot], ranks - 1)
            tree_solve(slot)
            xr[slot, me] = xb[slot, me]
            for n in range(len(offsets)):
                plane, column = peer(n)
                remote(
                    xb.at[slot, plane * 2 + column],
                    xr.at[slot, me],
                    xa_s.at[slot],
                    xa_r.at[slot, lax.div(me, NV)],
                    plane_device(plane, column),
                ).start()

        def unmerge(step, carry):
            @pl.when(lax.div(me, NV) == step)
            def _():
                group_recv(xr.at[slot], xa_r.at[slot, step], NV - 1)

            @pl.when(lax.div(me, NV) != step)
            def _():
                group_recv(xr.at[slot], xa_r.at[slot, step], NV)

            a_cross, a_last, b_first, b_cross, d = (gm[1, step, n] for n in range(5))
            for v in range(NV):
                xl, xh = xr[slot, step * NV + v, 0], xr[slot, step * NV + v, 1]
                _, b_head = by_core(pb[slot, mine + step, v, 0], pr[slot, step, v, 0])
                a_tail, _ = by_core(pb[slot, mine + step, v, 1], pr[slot, step, v, 1])
                mid_a, mid_b = inner_pair(a_tail + a_cross * xl, b_head + b_cross * xh, a_last, b_first, d)
                xx[slot, mine + step, v, 0] = jnp.where(core0, xl, mid_a)
                xx[slot, mine + step, v, 1] = jnp.where(core0, mid_b, xh)
                res[slot, step, v, 0] = jnp.where(core0, mid_a, xl)
                res[slot, step, v, 1] = jnp.where(core0, xh, mid_b)
            back_copy(slot, step).start()
            return carry

        lax.fori_loop(0, HALF, unmerge, 0)
        return q_halo

    def sweep(slot, t, v):
        low, high = xx[slot, t, v, 0], xx[slot, t, v, 1]
        values = [None] * ROWS
        later = high
        for i in range(ROWS - 1, -1, -1):
            later = yy[v, i, tile(t)] + cp[i, tile(t)] * low + cc[i, tile(t)] * later
            values[i] = later
        return low, high, values

    ax_halo.wait_recv()
    q_halo = section(0)
    for copy in q_halo:
        copy.wait_recv()

    def update_one(t, carry):
        diag_low = 2.0 + inverse_smoothing(rad[0, tile(t)])
        diag_high = 2.0 + inverse_smoothing(rad[ROWS + 1, tile(t)])
        for v in range(NV):
            low, high, values = sweep(0, t, v)
            low2 = diag_low * low - values[0] - qhalo[0, v, tile(t)]
            high2 = diag_high * high - values[ROWS - 1] - qhalo[1, v, tile(t)]
            for i, value in enumerate([low2, low] + values + [high, high2]):
                u2[v, i, tile(t)] = u1[v, i, tile(t)] + SECTION_ONE * dt[i, tile(t)] * value
        return pack(u2, t, carry)

    def update_one_late(step, carry):
        arrival(0, step).wait_recv()
        return update_one(other + step, carry)

    packed = lax.fori_loop(0, HALF, lambda step, carry: update_one(mine + step, carry), blank)
    packed = lax.fori_loop(0, HALF, update_one_late, packed)
    keep_packed(1, packed)
    ax_halo = Axial(axial_pair(1)).start()
    lax.fori_loop(0, TILES, functools.partial(local_step, u2, 1), 0)
    ax_halo.wait_recv()
    section(1)

    def update_two(t, carry):
        for v in range(NV):
            _, _, values = sweep(1, t, v)
            for i, value in enumerate(values):
                start = pl.multiple_of((v * TILES + t) * (SUB * ROWS), SUB) + i
                out[pl.ds(start, SUB, stride=ROWS), :] = u1[v, i + 2, tile(t)] + dt[i + 2, tile(t)] * value
        return carry

    def update_two_late(step, carry):
        arrival(1, step).wait_recv()
        return update_two(other + step, carry)

    lax.fori_loop(0, HALF, lambda step, carry: update_two(mine + step, carry), 0)
    lax.fori_loop(0, HALF, update_two_late, 0)
    section_sent(1)


def solution(mesh):
    count = mesh.shape["blk"]
    nz, na = count // 4, mesh.shape["axial"]
    split = Mesh(mesh.devices.reshape(nz, 2, 2, na), (*BLK, "axial"))
    ranks = nz * 2

    def on_device(fields, inv_volume, radius_ratio, time_step, jac_circ, jac_other):
        layers = fields.shape[1]
        vmem = lambda *shape: pltpu.VMEM(shape, F32)
        dma = lambda *shape: pltpu.SemaphoreType.DMA(shape)
        plane = (layers, LANES)
        cell = (SUB, LANES)
        scratch = [
            vmem(NV, ROWS + 4, *plane),
            vmem(NV, ROWS + 4, *plane),
            vmem(ROWS, *plane),
            vmem(ROWS + 2, *plane),
            vmem(ROWS + 4, *plane),
            vmem(ROWS, *plane),
            vmem(ROWS, *plane),
            vmem(ROWS, *plane),
            vmem(NV, ROWS, *plane),
            vmem(2, NV, *plane),
            vmem(2, NV, *plane),
            vmem(2, 2, NV, *cell),
            vmem(2, 2, NV, *cell),
            vmem(2, TILES, NV, 2, *cell),
            vmem(2, HALF, NV, 2, *cell),
            vmem(2, UNITS, 2, *cell),
            vmem(2, ranks, 2, *cell),
            vmem(2, ranks, 2, *cell),
            vmem(2, UNITS, 2, *cell),
            vmem(2, TILES, NV, 2, *cell),
            vmem(TILES, 3, *cell),
            vmem(HALF, 3, *cell),
            vmem(2, HALF, 5, *cell),
            vmem(ranks, 3, *cell),
            vmem(2 * ranks, 4, *cell),
            vmem(2 * ranks, 2, *cell),
            vmem(2 * ranks, 2, *cell),
            vmem(2, HALF, NV, 2, *cell),
            vmem(3, NV, NV, *cell),
            vmem(2, NV, *cell),
            dma(5),
            dma(2, TILES),
            dma(2, TILES),
            dma(2, 2),
            dma(2, 2),
            dma(2, 2),
            dma(2, 2),
            dma(2),
            dma(2),
            pltpu.SemaphoreType.DMA,
            pltpu.SemaphoreType.DMA,
            pltpu.SemaphoreType.DMA,
            pltpu.SemaphoreType.DMA,
            dma(2, HALF),
            dma(2, HALF),
            dma(2),
            dma(2),
            dma(2),
            dma(2, HALF),
            dma(2, HALF),
            dma(2, HALF),
            pltpu.SemaphoreType.REGULAR((3,)),
        ]
        anywhere = pl.BlockSpec(memory_space=pl.ANY)
        scalars = pl.BlockSpec(memory_space=pltpu.SMEM)
        rows = fields.shape[0] * layers * fields.shape[2]
        operands = (fields, inv_volume, radius_ratio, time_step, jac_circ, jnp.transpose(jac_other, (1, 0, 2)))
        result = pl.pallas_call(
            functools.partial(kernel, nz, na),
            out_shape=jax.ShapeDtypeStruct((rows, LANES), F32),
            in_specs=[anywhere] * 4 + [scalars] * 2,
            out_specs=pl.BlockSpec(memory_space=pltpu.VMEM),
            scratch_shapes=scratch,
            compiler_params=pltpu.CompilerParams(
                collective_id=0, has_side_effects=True, vmem_limit_bytes=24 * 1024 * 1024
            ),
        )(*(pltpu.with_memory_space_constraint(x, pltpu.HBM) for x in operands))
        return result.reshape(fields.shape)

    return jax.shard_map(
        on_device,
        mesh=split,
        in_specs=(
            P(None, None, BLK, "axial"),
            P(None, BLK, "axial"),
            P(None, BLK, "axial"),
            P(None, BLK, "axial"),
            P(),
            P(),
        ),
        out_specs=P(None, None, BLK, "axial"),
        check_vma=False,
    )
```
